512 devices in a mesh: grp: 16 (over y, x), sp: 32 (over z, core).
Axes of the slice: x: 4, y: 4, z: 16, core: 2. Of those that a mesh axis runs over, the one named last changes fastest.
Arguments:
- coarse: bfloat16 [1024, 48, 1024], P(('grp', 'sp')), parts along dimension 0, may hold values from -30 to 30
- conv_weight: bfloat16 [1024, 3, 3, 1024], P('sp'), may hold values from -0.104166667 to 0.104166667
- conv_bias: float32 [1024], P('sp'), may hold values from -5 to 5
- norm_gain: float32 [1024], P('sp'), may hold values from 0.5 to 1.5
- norm_shift: float32 [1024], P('sp'), may hold values from -3 to 3
- up_weight: bfloat16 [512, 2, 2, 1024], P('sp'), may hold values from -0.1875 to 0.1875
- up_bias: bfloat16 [512], P('sp'), may hold values from -3 to 3
Outputs:
- fine: bfloat16 [2048, 96, 512], P(('grp', 'sp')), parts along dimension 0
The draws below stay inside these ranges and needn't reach their ends.
There are 16 independent parts, one for each index of `grp`. The reference program is written for one: setup_inputs(seed, part) draws one part's arguments, and reference() takes and returns one part's arrays. A program takes and returns all parts, laid end to end along the dimension named above; an argument that names none is the same for every part. Nothing has to cross between parts.
All inputs are finite; a program needn't handle non-finite values.
Results may differ from the reference program's by a relative error of at most 0.0042.
Values may be sent and summed in bfloat16 or wider, within the bound.
No kernel may reach another device: no remote copies, remote signals or barrier semaphores. Data moves between devices by JAX's collectives and lax.ppermute only.
A program may use at most 64 MiB of HBM per device.

```python
import math
import jax
import jax.numpy as jnp
from jax import lax

CH = 1024
OUT = 512
GSIZE = 32
COLS = 48
HEIGHT = 64


def draw_coarse(key, part):
    first, second, third = jax.random.split(key, 3)
    pixel = jnp.exp(jax.random.uniform(second, (HEIGHT, COLS, 1), jnp.float32, math.log(0.3), math.log(3.0)))
    channel = jnp.exp(jax.random.uniform(third, (1, 1, CH), jnp.float32, math.log(0.5), math.log(2.0)))
    values = jax.random.normal(first, (HEIGHT, COLS, CH), jnp.float32)
    values = jnp.clip(values, -5.0, 5.0)
    return (values * pixel * channel).astype(jnp.bfloat16)


def draw_conv_weight(key, part):
    first, second = jax.random.split(key, 2)
    column = jnp.exp(jax.random.uniform(second, (CH, 1, 1, 1), jnp.float32, math.log(0.5), math.log(2.0)))
    values = jnp.clip(jax.random.normal(first, (CH, 3, 3, CH), jnp.float32), -5.0, 5.0)
    return (values * column * (9.0 * CH) ** (-0.5)).astype(jnp.bfloat16)


def levels(stream_key, shape, pieces, low, high):
    level = 1.0
    for axis_at, shards_of in pieces:
        steps = jax.random.uniform(jax.random.fold_in(jax.random.fold_in(stream_key, 6), axis_at), (shards_of,), jnp.float32, low / len(pieces), high / len(pieces))
        level = level * jnp.repeat(jnp.exp(steps), shape[axis_at] // shards_of).reshape((-1,) + (1,) * (len(shape) - 1 - axis_at))
    return level


def gaussian(stream_key, shape, deviation, bound, pieces=(), dtype=jnp.bfloat16):
    result = deviation * jax.random.normal(stream_key, shape, jnp.float32)
    if pieces:
        result = result * levels(stream_key, shape, pieces, -0.22, 0.18)
    return jnp.clip(result, -bound, bound).astype(dtype)


def setup_inputs(seed: int = 0, part: int = 0) -> dict:
    splits = jax.random.split(jax.random.key(seed), 8)
    part_splits = jax.random.split(jax.random.fold_in(splits[7], part), 8)
    return {
        "coarse": draw_coarse(jax.random.fold_in(jax.random.fold_in(splits[7], part), 71), part),
        "conv_weight": draw_conv_weight(jax.random.fold_in(splits[7], 71), part),
        "conv_bias": gaussian(splits[2], (CH,), 1.0, 5.0, ((0, 32),), jnp.float32),
        "norm_gain": jnp.clip(1.0 + 0.1 * jax.random.normal(splits[3], (CH,), jnp.float32), 0.5, 1.5),
        "norm_shift": gaussian(splits[4], (CH,), 0.5, 3.0, ((0, 32),), jnp.float32),
        "up_weight": gaussian(splits[5], (OUT, 2, 2, CH), CH ** -0.5, 0.1875, ((0, 32),)),
        "up_bias": gaussian(splits[6], (OUT,), 0.5, 3.0, ((0, 32),)),
    }


def reference(coarse, conv_weight, conv_bias, norm_gain, norm_shift, up_weight, up_bias):
    image = coarse.astype(jnp.float32)[None]
    kernel = jnp.transpose(conv_weight.astype(jnp.float32), (1, 2, 3, 0))
    convolved = lax.conv_general_dilated(image, kernel, (1, 1), 'SAME', dimension_numbers=('NHWC', 'HWIO', 'NHWC'), precision=lax.Precision.HIGHEST)[0]
    convolved = convolved + conv_bias
    grouped = convolved.reshape(HEIGHT, COLS, CH // GSIZE, GSIZE)
    centre = lax.optimization_barrier(jnp.mean(grouped, axis=(0, 1, 3), keepdims=True))
    spread = lax.optimization_barrier(jnp.mean(jnp.square(grouped - centre), axis=(0, 1, 3), keepdims=True))
    normed = ((grouped - centre) * lax.rsqrt(spread + 1e-05)).reshape(HEIGHT, COLS, CH)
    activated = jax.nn.silu(normed * norm_gain + norm_shift).astype(jnp.bfloat16)
    decoded = jnp.einsum('ijc,oabc->iajbo', activated.astype(jnp.float32), up_weight.astype(jnp.float32), precision=lax.Precision.HIGHEST)
    decoded = decoded.reshape(2 * HEIGHT, 2 * COLS, OUT) + up_bias
    return decoded.astype(jnp.bfloat16)
```

```python
import jax
import jax.numpy as jnp
from jax import lax
from jax.sharding import Mesh, PartitionSpec as P

GSIZE = 32


def gather_rows(local, axis):
    by_z = lax.all_gather(local, "z", axis=0, tiled=False)
    both = lax.all_gather(by_z, "core", axis=1, tiled=False)
    return both.reshape((-1,) + local.shape[1:])


def normalize(convolved, norm_gain, norm_shift):
    height, width_cols, outputs = convolved.shape
    grouped = convolved.reshape(height, width_cols, outputs // GSIZE, GSIZE)
    centre = jnp.mean(grouped, axis=(0, 1, 3), keepdims=True)
    spread = jnp.mean(jnp.square(grouped - centre), axis=(0, 1, 3), keepdims=True)
    normed = ((grouped - centre) * lax.rsqrt(spread + 1e-05)).reshape(height, width_cols, outputs)
    return jax.nn.silu(normed * norm_gain + norm_shift).astype(jnp.bfloat16)


def body(coarse, conv_weight, conv_bias, norm_gain, norm_shift, up_weight, up_bias):
    whole = gather_rows(coarse, 0)
    up_weight, up_bias, whole = lax.optimization_barrier((up_weight, up_bias, whole))
    convolved = lax.conv_general_dilated(
        whole[None],
        conv_weight,
        (1, 1),
        "SAME",
        dimension_numbers=("NHWC", "OHWI", "NHWC"),
        preferred_element_type=jnp.float32,
    )[0]
    activated = normalize(convolved + conv_bias, norm_gain, norm_shift)
    slice_out = up_weight.shape[0]
    flat = up_weight.reshape(slice_out, -1)
    packed = jnp.concatenate([flat, jnp.pad(up_bias[:, None], ((0, 0), (0, 127)))], axis=1)
    packed_all = lax.all_gather(packed, ("z", "core"), axis=0, tiled=True)
    weight_all = packed_all[:, : flat.shape[1]].reshape((-1,) + up_weight.shape[1:])
    bias_all = packed_all[:, flat.shape[1]]
    rows = lax.all_to_all(activated, ("z", "core"), split_axis=0, concat_axis=2, tiled=True)
    decoded = jnp.einsum("ijc,oabc->iajbo", rows, weight_all, preferred_element_type=jnp.float32)
    decoded = decoded + bias_all.astype(jnp.float32)
    height, _, width_cols, _, outputs = decoded.shape
    return decoded.astype(jnp.bfloat16).reshape(2 * height, 2 * width_cols, outputs)


def solution(mesh):
    grp, sp = mesh.devices.shape
    fine_mesh = Mesh(mesh.devices.reshape(grp, sp // 2, 2), ("grp", "z", "core"))
    rows = ("grp", "z", "core")
    chans = ("z", "core")
    return jax.shard_map(
        body,
        mesh=fine_mesh,
        in_specs=(
            P(rows, None, None),
            P(chans, None, None, None),
            P(chans),
            P(chans),
            P(chans),
            P(chans, None, None, None),
            P(chans),
        ),
        out_specs=P(rows, None, None),
        check_vma=False,
    )
```

```python
import jax
import jax.numpy as jnp
from jax import lax
from jax.sharding import Mesh, PartitionSpec as P

GSIZE = 32


def conv_rows(weights_cat, width_cols, channels, outputs, tile_rows):
    how_many = tile_rows.shape[0]
    padded = jnp.pad(tile_rows, ((0, 0), (1, 1), (0, 0)))
    partial_sum = jnp.zeros((how_many * width_cols, 3 * outputs), jnp.float32)
    for offset in range(3):
        window = padded[:, offset : offset + width_cols, :].reshape(how_many * width_cols, channels)
        partial_sum = partial_sum + jnp.dot(
            window, weights_cat[offset], preferred_element_type=jnp.float32
        )
    partial_sum = partial_sum.reshape(how_many, width_cols, 3, outputs)
    contrib = jnp.zeros((how_many + 2, width_cols, outputs), jnp.float32)
    for kernel_row in range(3):
        contrib = contrib.at[2 - kernel_row : 2 - kernel_row + how_many].add(
            partial_sum[:, :, kernel_row]
        )
    return contrib


def normalize(convolved, norm_gain, norm_shift):
    height, width_cols, outputs = convolved.shape
    grouped = convolved.reshape(height, width_cols, outputs // GSIZE, GSIZE)
    centre = jnp.mean(grouped, axis=(0, 1, 3), keepdims=True)
    spread = jnp.mean(jnp.square(grouped - centre), axis=(0, 1, 3), keepdims=True)
    normed = ((grouped - centre) * lax.rsqrt(spread + 1e-05)).reshape(height, width_cols, outputs)
    return jax.nn.silu(normed * norm_gain + norm_shift).astype(jnp.bfloat16)


def body(coarse, conv_weight, conv_bias, norm_gain, norm_shift, up_weight, up_bias):
    chips = lax.axis_size("z")
    core = lax.axis_index("core")
    _, width_cols, channels = coarse.shape
    outputs = conv_weight.shape[0]
    slice_out = up_weight.shape[0]

    whole = lax.all_gather(coarse, ("z", "core"), axis=0, tiled=True)
    height = whole.shape[0]
    flat = up_weight.reshape(slice_out, -1)
    packed = jnp.concatenate([flat, jnp.pad(up_bias[:, None], ((0, 0), (0, 127)))], axis=1)
    packed, whole = lax.optimization_barrier((packed, whole))
    packed_z = lax.all_gather(packed, "z", axis=0, tiled=False)
    weight_half = packed_z[:, :, : flat.shape[1]].reshape((chips, slice_out) + up_weight.shape[1:])
    bias_half = packed_z[:, :, flat.shape[1]].astype(jnp.float32)

    weights_cat = jnp.transpose(conv_weight, (2, 3, 1, 0)).reshape(3, channels, 3 * outputs)
    summed = conv_rows(weights_cat, width_cols, channels, outputs, whole)
    activated = normalize(summed[1 : height + 1] + conv_bias, norm_gain, norm_shift)

    chip_rows = lax.all_to_all(activated, "z", split_axis=0, concat_axis=2, tiled=True)
    both = lax.all_gather(chip_rows, "core", axis=0, tiled=False)
    local_rows = chip_rows.shape[0]
    both = both.reshape(2, local_rows, width_cols, chips, outputs)
    act = jnp.transpose(both, (1, 2, 3, 0, 4)).reshape(local_rows, width_cols, chips * 2 * outputs)

    decoded = jnp.einsum("ijc,zoabc->iajbzo", act, weight_half, preferred_element_type=jnp.float32)
    decoded = (decoded + bias_half).astype(jnp.bfloat16)
    half = local_rows // 2
    own = lax.dynamic_slice_in_dim(decoded, core * half, half, axis=0)
    other = lax.dynamic_slice_in_dim(decoded, (1 - core) * half, half, axis=0)
    received = lax.ppermute(other, "core", [(0, 1), (1, 0)])
    low = jnp.where(core == 0, own, received)
    high = jnp.where(core == 0, received, own)
    fine = jnp.stack([low, high], axis=5)
    return fine.reshape(2 * half, 2 * width_cols, chips * 2 * slice_out)


def solution(mesh):
    grp, sp = mesh.devices.shape
    fine_mesh = Mesh(mesh.devices.reshape(grp, sp // 2, 2), ("grp", "z", "core"))
    rows = ("grp", "z", "core")
    chans = ("z", "core")
    return jax.shard_map(
        body,
        mesh=fine_mesh,
        in_specs=(
            P(rows, None, None),
            P(chans, None, None, None),
            P(chans),
            P(chans),
            P(chans),
            P(chans, None, None, None),
            P(chans),
        ),
        out_specs=P(rows, None, None),
        check_vma=False,
    )
```

```python
import jax
import jax.numpy as jnp
from jax import lax
from jax.sharding import Mesh, PartitionSpec as P

GSIZE = 32


def conv_rows(weights_cat, width_cols, channels, outputs, tile_rows):
    how_many = tile_rows.shape[0]
    padded = jnp.pad(tile_rows, ((0, 0), (1, 1), (0, 0)))
    partial_sum = jnp.zeros((how_many * width_cols, 3 * outputs), jnp.float32)
    for offset in range(3):
        window = padded[:, offset : offset + width_cols, :].reshape(how_many * width_cols, channels)
        partial_sum = partial_sum + jnp.dot(
            window, weights_cat[offset], preferred_element_type=jnp.float32
        )
    partial_sum = partial_sum.reshape(how_many, width_cols, 3, outputs)
    contrib = jnp.zeros((how_many + 2, width_cols, outputs), jnp.float32)
    for kernel_row in range(3):
        contrib = contrib.at[2 - kernel_row : 2 - kernel_row + how_many].add(
            partial_sum[:, :, kernel_row]
        )
    return contrib


def ring_gather(block, axis):
    chips = lax.axis_size(axis)
    step_up = [(i, (i - 1) % chips) for i in range(chips)]
    step_down = [(i, (i + 1) % chips) for i in range(chips)]
    ahead, behind = block, block
    from_ahead, from_behind = [], []
    for k in range(1, chips // 2 + 1):
        ahead = lax.ppermute(ahead, axis, step_up)
        from_ahead.append(ahead)
        if k < chips - chips // 2:
            behind = lax.ppermute(behind, axis, step_down)
            from_behind.append(behind)
    stacked = jnp.stack([block] + from_ahead + from_behind[::-1])
    return jnp.roll(stacked, lax.axis_index(axis), axis=0)


def normalize(convolved, norm_gain, norm_shift):
    height, width_cols, outputs = convolved.shape
    grouped = convolved.reshape(height, width_cols, outputs // GSIZE, GSIZE)
    centre = jnp.mean(grouped, axis=(0, 1, 3), keepdims=True)
    spread = jnp.mean(jnp.square(grouped - centre), axis=(0, 1, 3), keepdims=True)
    normed = ((grouped - centre) * lax.rsqrt(spread + 1e-05)).reshape(height, width_cols, outputs)
    return jax.nn.silu(normed * norm_gain + norm_shift).astype(jnp.bfloat16)


def body(coarse, conv_weight, conv_bias, norm_gain, norm_shift, up_weight, up_bias):
    chips = lax.axis_size("z")
    core = lax.axis_index("core")
    _, width_cols, channels = coarse.shape
    outputs = conv_weight.shape[0]
    slice_out = up_weight.shape[0]

    whole = lax.all_gather(coarse, ("z", "core"), axis=0, tiled=True)
    height = whole.shape[0]
    flat = up_weight.reshape(slice_out, -1)
    packed = jnp.concatenate([flat, jnp.pad(up_bias[:, None], ((0, 0), (0, 127)))], axis=1)
    packed_z = ring_gather(packed, "z")
    weight_half = packed_z[:, :, : flat.shape[1]].reshape((chips, slice_out) + up_weight.shape[1:])
    bias_half = packed_z[:, :, flat.shape[1]].astype(jnp.float32)

    weights_cat = jnp.transpose(conv_weight, (2, 3, 1, 0)).reshape(3, channels, 3 * outputs)
    summed = conv_rows(weights_cat, width_cols, channels, outputs, whole)
    activated = normalize(summed[1 : height + 1] + conv_bias, norm_gain, norm_shift)

    chip_rows = lax.all_to_all(activated, "z", split_axis=0, concat_axis=2, tiled=True)
    both = lax.all_gather(chip_rows, "core", axis=0, tiled=False)
    local_rows = chip_rows.shape[0]
    both = both.reshape(2, local_rows, width_cols, chips, outputs)
    act = jnp.transpose(both, (1, 2, 3, 0, 4)).reshape(local_rows, width_cols, chips * 2 * outputs)

    decoded = jnp.einsum("ijc,zoabc->iajbzo", act, weight_half, preferred_element_type=jnp.float32)
    decoded = (decoded + bias_half).astype(jnp.bfloat16)
    half = local_rows // 2
    own = lax.dynamic_slice_in_dim(decoded, core * half, half, axis=0)
    other = lax.dynamic_slice_in_dim(decoded, (1 - core) * half, half, axis=0)
    received = lax.ppermute(other, "core", [(0, 1), (1, 0)])
    low = jnp.where(core == 0, own, received)
    high = jnp.where(core == 0, received, own)
    fine = jnp.stack([low, high], axis=5)
    return fine.reshape(2 * half, 2 * width_cols, chips * 2 * slice_out)


def solution(mesh):
    grp, sp = mesh.devices.shape
    fine_mesh = Mesh(mesh.devices.reshape(grp, sp // 2, 2), ("grp", "z", "core"))
    rows = ("grp", "z", "core")
    chans = ("z", "core")
    return jax.shard_map(
        body,
        mesh=fine_mesh,
        in_specs=(
            P(rows, None, None),
            P(chans, None, None, None),
            P(chans),
            P(chans),
            P(chans),
            P(chans, None, None, None),
            P(chans),
        ),
        out_specs=P(rows, None, None),
        check_vma=False,
    )
```

```python
import functools

import jax
import jax.numpy as jnp
from jax import lax
from jax.experimental import pallas as pl
from jax.experimental.pallas import tpu as pltpu
from jax.sharding import Mesh, PartitionSpec as P

GSIZE = 32


def conv_norm_kernel(x_ref, w_ref, bias_ref, gain_ref, shift_ref, out_ref, *, height, width_cols):
    outputs = out_ref.shape[0]
    positions = height * width_cols
    taps = lax.dot_general(w_ref[...], x_ref[...], (((1,), (1,)), ((), ())),
                           preferred_element_type=jnp.float32)
    pos = lax.broadcasted_iota(jnp.int32, (1, positions), 1)
    row = pos // width_cols
    col = pos % width_cols
    acc = jnp.zeros((outputs, positions), jnp.float32)
    for t in range(9):
        r, s = divmod(t, 3)
        off = (r - 1) * width_cols + (s - 1)
        part = taps[t * outputs:(t + 1) * outputs, :]
        if off:
            part = pltpu.roll(part, (-off) % positions, 1)
        valid = ((row + (r - 1) >= 0) & (row + (r - 1) < height)
                 & (col + (s - 1) >= 0) & (col + (s - 1) < width_cols))
        acc = acc + jnp.where(valid, part, 0.0)
    conv = acc + bias_ref[...]
    groups = outputs // GSIZE
    grouped = conv.reshape(groups, GSIZE, positions)
    count = GSIZE * positions
    centre = jnp.sum(jnp.sum(grouped, axis=2, keepdims=True), axis=1, keepdims=True) / count
    dev = grouped - centre
    spread = jnp.sum(jnp.sum(dev * dev, axis=2, keepdims=True), axis=1, keepdims=True) / count
    normed = (dev * lax.rsqrt(spread + 1e-05)).reshape(outputs, positions)
    v = normed * gain_ref[...] + shift_ref[...]
    out_ref[...] = (v / (1.0 + jnp.exp(-v))).astype(out_ref.dtype)


def conv_norm(whole, conv_weight, conv_bias, norm_gain, norm_shift):
    height, width_cols, channels = whole.shape
    outputs = conv_weight.shape[0]
    x = whole.reshape(height * width_cols, channels)
    w = jnp.transpose(conv_weight.reshape(outputs, 9, channels), (1, 0, 2)).reshape(9 * outputs, channels)
    col = lambda v: v.astype(jnp.float32).reshape(outputs, 1)
    vmem = pl.BlockSpec(memory_space=pltpu.VMEM)
    return pl.pallas_call(
        functools.partial(conv_norm_kernel, height=height, width_cols=width_cols),
        out_shape=jax.ShapeDtypeStruct((outputs, height * width_cols), jnp.bfloat16),
        in_specs=[vmem] * 5,
        out_specs=vmem,
        cost_estimate=pl.CostEstimate(
            flops=2 * height * width_cols * channels * 9 * outputs,
            transcendentals=height * width_cols * outputs,
            bytes_accessed=x.size * 2 + w.size * 2 + outputs * height * width_cols * 2),
    )(x, w, col(conv_bias), col(norm_gain), col(norm_shift))


def ring_gather(block, axis):
    chips = lax.axis_size(axis)
    step_up = [(i, (i - 1) % chips) for i in range(chips)]
    step_down = [(i, (i + 1) % chips) for i in range(chips)]
    ahead, behind = block, block
    from_ahead, from_behind = [], []
    for k in range(1, chips // 2 + 1):
        ahead = lax.ppermute(ahead, axis, step_up)
        from_ahead.append(ahead)
        if k < chips - chips // 2:
            behind = lax.ppermute(behind, axis, step_down)
            from_behind.append(behind)
    stacked = jnp.stack([block] + from_ahead + from_behind[::-1])
    return jnp.roll(stacked, lax.axis_index(axis), axis=0)


def body(coarse, conv_weight, conv_bias, norm_gain, norm_shift, up_weight, up_bias):
    chips = lax.axis_size("z")
    core = lax.axis_index("core")
    _, width_cols, channels = coarse.shape
    outputs = conv_weight.shape[0]
    slice_out = up_weight.shape[0]

    whole = lax.all_gather(coarse, ("z", "core"), axis=0, tiled=True)
    height = whole.shape[0]
    flat = up_weight.reshape(slice_out, -1)
    packed = jnp.concatenate([flat, jnp.pad(up_bias[:, None], ((0, 0), (0, 127)))], axis=1)
    packed_z = ring_gather(packed, "z")
    weight_half = packed_z[:, :, : flat.shape[1]].reshape((chips, slice_out) + up_weight.shape[1:])
    bias_half = packed_z[:, :, flat.shape[1]].astype(jnp.float32)

    activated = conv_norm(whole, conv_weight, conv_bias, norm_gain, norm_shift)
    activated = jnp.transpose(activated).reshape(height, width_cols, outputs)

    chip_rows = lax.all_to_all(activated, "z", split_axis=0, concat_axis=2, tiled=True)
    both = lax.all_gather(chip_rows, "core", axis=0, tiled=False)
    local_rows = chip_rows.shape[0]
    both = both.reshape(2, local_rows, width_cols, chips, outputs)
    act = jnp.transpose(both, (1, 2, 3, 0, 4)).reshape(local_rows, width_cols, chips * 2 * outputs)

    decoded = jnp.einsum("ijc,zoabc->iajbzo", act, weight_half, preferred_element_type=jnp.float32)
    decoded = (decoded + bias_half).astype(jnp.bfloat16)
    half = local_rows // 2
    own = lax.dynamic_slice_in_dim(decoded, core * half, half, axis=0)
    other = lax.dynamic_slice_in_dim(decoded, (1 - core) * half, half, axis=0)
    received = lax.ppermute(other, "core", [(0, 1), (1, 0)])
    low = jnp.where(core == 0, own, received)
    high = jnp.where(core == 0, received, own)
    fine = jnp.stack([low, high], axis=5)
    return fine.reshape(2 * half, 2 * width_cols, chips * 2 * slice_out)


def solution(mesh):
    grp, sp = mesh.devices.shape
    fine_mesh = Mesh(mesh.devices.reshape(grp, sp // 2, 2), ("grp", "z", "core"))
    rows = ("grp", "z", "core")
    chans = ("z", "core")
    return jax.shard_map(
        body,
        mesh=fine_mesh,
        in_specs=(
            P(rows, None, None),
            P(chans, None, None, None),
            P(chans),
            P(chans),
            P(chans),
            P(chans, None, None, None),
            P(chans),
        ),
        out_specs=P(rows, None, None),
        check_vma=False,
    )
```

```python
import functools

import jax
import jax.numpy as jnp
from jax import lax
from jax.experimental import pallas as pl
from jax.experimental.pallas import tpu as pltpu
from jax.sharding import Mesh, PartitionSpec as P

GSIZE = 32


def conv_norm_kernel(x_ref, w_ref, bias_ref, gain_ref, shift_ref, out_ref, *, height, width_cols):
    outputs = out_ref.shape[0]
    positions = height * width_cols
    taps = lax.dot_general(w_ref[...], x_ref[...], (((1,), (1,)), ((), ())),
                           preferred_element_type=jnp.float32)
    pos = lax.broadcasted_iota(jnp.int32, (1, positions), 1)
    row = pos // width_cols
    col = pos % width_cols
    acc = jnp.zeros((outputs, positions), jnp.float32)
    for t in range(9):
        r, s = divmod(t, 3)
        off = (r - 1) * width_cols + (s - 1)
        part = taps[t * outputs:(t + 1) * outputs, :]
        if off:
            part = pltpu.roll(part, (-off) % positions, 1)
        valid = ((row + (r - 1) >= 0) & (row + (r - 1) < height)
                 & (col + (s - 1) >= 0) & (col + (s - 1) < width_cols))
        acc = acc + jnp.where(valid, part, 0.0)
    conv = acc + bias_ref[...]
    groups = outputs // GSIZE
    grouped = conv.reshape(groups, GSIZE, positions)
    count = GSIZE * positions
    centre = jnp.sum(jnp.sum(grouped, axis=2, keepdims=True), axis=1, keepdims=True) / count
    dev = grouped - centre
    spread = jnp.sum(jnp.sum(dev * dev, axis=2, keepdims=True), axis=1, keepdims=True) / count
    normed = (dev * lax.rsqrt(spread + 1e-05)).reshape(outputs, positions)
    v = normed * gain_ref[...] + shift_ref[...]
    out_ref[...] = (v / (1.0 + jnp.exp(-v))).astype(out_ref.dtype)


def conv_norm(whole, conv_weight, conv_bias, norm_gain, norm_shift):
    height, width_cols, channels = whole.shape
    outputs = conv_weight.shape[0]
    x = whole.reshape(height * width_cols, channels)
    w = jnp.transpose(conv_weight.reshape(outputs, 9, channels), (1, 0, 2)).reshape(9 * outputs, channels)
    col = lambda v: v.astype(jnp.float32).reshape(outputs, 1)
    vmem = pl.BlockSpec(memory_space=pltpu.VMEM)
    return pl.pallas_call(
        functools.partial(conv_norm_kernel, height=height, width_cols=width_cols),
        out_shape=jax.ShapeDtypeStruct((outputs, height * width_cols), jnp.bfloat16),
        in_specs=[vmem] * 5,
        out_specs=vmem,
        cost_estimate=pl.CostEstimate(
            flops=2 * height * width_cols * channels * 9 * outputs,
            transcendentals=height * width_cols * outputs,
            bytes_accessed=x.size * 2 + w.size * 2 + outputs * height * width_cols * 2),
    )(x, w, col(conv_bias), col(norm_gain), col(norm_shift))


def ring_gather(block, axis):
    chips = lax.axis_size(axis)
    step_up = [(i, (i - 1) % chips) for i in range(chips)]
    step_down = [(i, (i + 1) % chips) for i in range(chips)]
    ahead, behind = block, block
    from_ahead, from_behind = [], []
    for k in range(1, chips // 2 + 1):
        ahead = lax.ppermute(ahead, axis, step_up)
        from_ahead.append(ahead)
        if k < chips - chips // 2:
            behind = lax.ppermute(behind, axis, step_down)
            from_behind.append(behind)
    stacked = jnp.stack([block] + from_ahead + from_behind[::-1])
    return jnp.roll(stacked, lax.axis_index(axis), axis=0)


def body(coarse, conv_weight, conv_bias, norm_gain, norm_shift, up_weight, up_bias):
    chips = lax.axis_size("z")
    core = lax.axis_index("core")
    _, width_cols, channels = coarse.shape
    outputs = conv_weight.shape[0]
    slice_out = up_weight.shape[0]

    whole = lax.all_gather(coarse, ("z", "core"), axis=0, tiled=True)
    height = whole.shape[0]
    flat = up_weight.reshape(slice_out, -1)
    packed = jnp.concatenate([flat, jnp.pad(up_bias[:, None], ((0, 0), (0, 127)))], axis=1)
    packed_z = ring_gather(packed, "z")
    packed_other = lax.ppermute(packed_z, "core", [(0, 1), (1, 0)])
    low = jnp.where(core == 0, packed_z, packed_other)
    high = jnp.where(core == 0, packed_other, packed_z)
    packed_all = jnp.stack([low, high], axis=1).reshape(chips * 2 * slice_out, -1)
    up_all = packed_all[:, : flat.shape[1]].reshape((chips * 2 * slice_out,) + up_weight.shape[1:])
    bias_all = packed_all[:, flat.shape[1]].astype(jnp.float32)
    up_all = up_all.reshape(up_all.shape[:3] + (chips, 2, outputs))
    up_all = jnp.transpose(up_all, (4, 3, 5, 1, 2, 0)).reshape(channels, 2, 2, -1)

    activated = conv_norm(whole, conv_weight, conv_bias, norm_gain, norm_shift)
    activated = jnp.transpose(activated).reshape(height, width_cols, outputs)

    chip_rows = lax.all_to_all(activated, "z", split_axis=0, concat_axis=2, tiled=True)
    both = lax.all_gather(chip_rows, "core", axis=2, tiled=True)
    half = chip_rows.shape[0] // 2
    own = lax.dynamic_slice_in_dim(both, core * half, half, axis=0)

    decoded = jnp.einsum("ijc,cabo->iajbo", own, up_all, preferred_element_type=jnp.float32)
    decoded = (decoded + bias_all).astype(jnp.bfloat16)
    return decoded.reshape(2 * half, 2 * width_cols, -1)


def solution(mesh):
    grp, sp = mesh.devices.shape
    fine_mesh = Mesh(mesh.devices.reshape(grp, sp // 2, 2), ("grp", "z", "core"))
    rows = ("grp", "z", "core")
    chans = ("z", "core")
    return jax.shard_map(
        body,
        mesh=fine_mesh,
        in_specs=(
            P(rows, None, None),
            P(chans, None, None, None),
            P(chans),
            P(chans),
            P(chans),
            P(chans, None, None, None),
            P(chans),
        ),
        out_specs=P(rows, None, None),
        check_vma=False,
    )
```

```python
import functools

import jax
import jax.numpy as jnp
from jax import lax
from jax.experimental import pallas as pl
from jax.experimental.pallas import tpu as pltpu
from jax.sharding import Mesh, PartitionSpec as P

GSIZE = 32


def conv_norm_kernel(x_ref, w_ref, bias_ref, gain_ref, shift_ref, out_ref, *, height, width_cols):
    outputs = out_ref.shape[0]
    positions = height * width_cols
    taps = lax.dot_general(w_ref[...], x_ref[...], (((1,), (1,)), ((), ())),
                           preferred_element_type=jnp.float32)
    pos = lax.broadcasted_iota(jnp.int32, (1, positions), 1)
    row = pos // width_cols
    col = pos % width_cols
    acc = jnp.zeros((outputs, positions), jnp.float32)
    for t in range(9):
        r, s = divmod(t, 3)
        off = (r - 1) * width_cols + (s - 1)
        part = taps[t * outputs:(t + 1) * outputs, :]
        if off:
            part = pltpu.roll(part, (-off) % positions, 1)
        valid = ((row + (r - 1) >= 0) & (row + (r - 1) < height)
                 & (col + (s - 1) >= 0) & (col + (s - 1) < width_cols))
        acc = acc + jnp.where(valid, part, 0.0)
    conv = acc + bias_ref[...]
    groups = outputs // GSIZE
    grouped = conv.reshape(groups, GSIZE, positions)
    count = GSIZE * positions
    centre = jnp.sum(jnp.sum(grouped, axis=2, keepdims=True), axis=1, keepdims=True) / count
    dev = grouped - centre
    spread = jnp.sum(jnp.sum(dev * dev, axis=2, keepdims=True), axis=1, keepdims=True) / count
    normed = (dev * lax.rsqrt(spread + 1e-05)).reshape(outputs, positions)
    v = normed * gain_ref[...] + shift_ref[...]
    out_ref[...] = (v / (1.0 + jnp.exp(-v))).astype(out_ref.dtype)


def conv_norm(whole, conv_weight, conv_bias, norm_gain, norm_shift):
    height, width_cols, channels = whole.shape
    outputs = conv_weight.shape[0]
    x = whole.reshape(height * width_cols, channels)
    w = jnp.transpose(conv_weight.reshape(outputs, 9, channels), (1, 0, 2)).reshape(9 * outputs, channels)
    col = lambda v: v.astype(jnp.float32).reshape(outputs, 1)
    vmem = pl.BlockSpec(memory_space=pltpu.VMEM)
    return pl.pallas_call(
        functools.partial(conv_norm_kernel, height=height, width_cols=width_cols),
        out_shape=jax.ShapeDtypeStruct((outputs, height * width_cols), jnp.bfloat16),
        in_specs=[vmem] * 5,
        out_specs=vmem,
        cost_estimate=pl.CostEstimate(
            flops=2 * height * width_cols * channels * 9 * outputs,
            transcendentals=height * width_cols * outputs,
            bytes_accessed=x.size * 2 + w.size * 2 + outputs * height * width_cols * 2),
    )(x, w, col(conv_bias), col(norm_gain), col(norm_shift))


def ring_gather_rows(local):
    chips = lax.axis_size("z")
    core = lax.axis_index("core")
    here = lax.axis_index("z")
    chip = lax.all_gather(local, "core", axis=0, tiled=True)
    n = chip.shape[0]
    whole = jnp.zeros((chips * n,) + chip.shape[1:], chip.dtype)
    whole = lax.dynamic_update_slice_in_dim(whole, chip, here * n, axis=0)
    walk = []
    for z in range(chips):
        walk.append((2 * z, 2 * ((z - 1) % chips)))
        walk.append((2 * z + 1, 2 * ((z + 1) % chips) + 1))
    swap = [(0, 1), (1, 0)]
    sign = 1 - 2 * core
    block = chip
    for k in range(1, chips // 2 + 1):
        block = lax.ppermute(block, ("z", "core"), walk)
        whole = lax.dynamic_update_slice_in_dim(whole, block, ((here + sign * k) % chips) * n, axis=0)
        if k < chips - chips // 2:
            other = lax.ppermute(block, "core", swap)
            whole = lax.dynamic_update_slice_in_dim(whole, other, ((here - sign * k) % chips) * n, axis=0)
    return whole


def body(coarse, conv_weight, conv_bias, norm_gain, norm_shift, up_weight, up_bias):
    chips = lax.axis_size("z")
    core = lax.axis_index("core")
    _, width_cols, channels = coarse.shape
    outputs = conv_weight.shape[0]
    slice_out = up_weight.shape[0]

    whole = ring_gather_rows(coarse)
    height = whole.shape[0]
    flat = up_weight.reshape(slice_out, -1)
    packed = jnp.concatenate([flat, jnp.pad(up_bias[:, None], ((0, 0), (0, 127)))], axis=1)
    packed_all = lax.all_gather(packed, ("z", "core"), axis=0, tiled=True)
    up_all = packed_all[:, : flat.shape[1]].reshape((chips * 2 * slice_out,) + up_weight.shape[1:])
    bias_all = packed_all[:, flat.shape[1]].astype(jnp.float32)

    activated = conv_norm(whole, conv_weight, conv_bias, norm_gain, norm_shift)
    activated = jnp.transpose(activated).reshape(height, width_cols, outputs)

    chip_rows = lax.all_to_all(activated, "z", split_axis=0, concat_axis=2, tiled=True)
    both = lax.all_gather(chip_rows, "core", axis=0, tiled=False)
    half = chip_rows.shape[0] // 2
    own = lax.dynamic_slice_in_dim(both, core * half, half, axis=1)
    own = own.reshape((2, half, width_cols, chips, outputs))
    own = jnp.transpose(own, (1, 2, 3, 0, 4)).reshape(half, width_cols, channels)

    decoded = jnp.einsum("ijc,oabc->iajbo", own, up_all, preferred_element_type=jnp.float32)
    decoded = (decoded + bias_all).astype(jnp.bfloat16)
    return decoded.reshape(2 * half, 2 * width_cols, -1)


def solution(mesh):
    grp, sp = mesh.devices.shape
    fine_mesh = Mesh(mesh.devices.reshape(grp, sp // 2, 2), ("grp", "z", "core"))
    rows = ("grp", "z", "core")
    chans = ("z", "core")
    return jax.shard_map(
        body,
        mesh=fine_mesh,
        in_specs=(
            P(rows, None, None),
            P(chans, None, None, None),
            P(chans),
            P(chans),
            P(chans),
            P(chans, None, None, None),
            P(chans),
        ),
        out_specs=P(rows, None, None),
        check_vma=False,
    )
```

```python
import functools

import jax
import jax.numpy as jnp
from jax import lax
from jax.experimental import pallas as pl
from jax.experimental.pallas import tpu as pltpu
from jax.sharding import Mesh, PartitionSpec as P

GSIZE = 32


def conv_norm_kernel(x_ref, w_ref, bias_ref, gain_ref, shift_ref, out_ref, *, height, width_cols):
    outputs = out_ref.shape[0]
    positions = height * width_cols
    taps = lax.dot_general(w_ref[...], x_ref[...], (((1,), (1,)), ((), ())),
                           preferred_element_type=jnp.float32)
    pos = lax.broadcasted_iota(jnp.int32, (1, positions), 1)
    row = pos // width_cols
    col = pos % width_cols
    acc = jnp.zeros((outputs, positions), jnp.float32)
    for t in range(9):
        r, s = divmod(t, 3)
        off = (r - 1) * width_cols + (s - 1)
        part = taps[t * outputs:(t + 1) * outputs, :]
        if off:
            part = pltpu.roll(part, (-off) % positions, 1)
        valid = ((row + (r - 1) >= 0) & (row + (r - 1) < height)
                 & (col + (s - 1) >= 0) & (col + (s - 1) < width_cols))
        acc = acc + jnp.where(valid, part, 0.0)
    conv = acc + bias_ref[...]
    groups = outputs // GSIZE
    grouped = conv.reshape(groups, GSIZE, positions)
    count = GSIZE * positions
    centre = jnp.sum(jnp.sum(grouped, axis=2, keepdims=True), axis=1, keepdims=True) / count
    dev = grouped - centre
    spread = jnp.sum(jnp.sum(dev * dev, axis=2, keepdims=True), axis=1, keepdims=True) / count
    normed = (dev * lax.rsqrt(spread + 1e-05)).reshape(outputs, positions)
    v = normed * gain_ref[...] + shift_ref[...]
    out_ref[...] = (v / (1.0 + jnp.exp(-v))).astype(out_ref.dtype)


def conv_norm(whole, conv_weight, conv_bias, norm_gain, norm_shift):
    height, width_cols, channels = whole.shape
    outputs = conv_weight.shape[0]
    x = whole.reshape(height * width_cols, channels)
    w = jnp.transpose(conv_weight.reshape(outputs, 9, channels), (1, 0, 2)).reshape(9 * outputs, channels)
    col = lambda v: v.astype(jnp.float32).reshape(outputs, 1)
    vmem = pl.BlockSpec(memory_space=pltpu.VMEM)
    return pl.pallas_call(
        functools.partial(conv_norm_kernel, height=height, width_cols=width_cols),
        out_shape=jax.ShapeDtypeStruct((outputs, height * width_cols), jnp.bfloat16),
        in_specs=[vmem] * 5,
        out_specs=vmem,
        cost_estimate=pl.CostEstimate(
            flops=2 * height * width_cols * channels * 9 * outputs,
            transcendentals=height * width_cols * outputs,
            bytes_accessed=x.size * 2 + w.size * 2 + outputs * height * width_cols * 2),
    )(x, w, col(conv_bias), col(norm_gain), col(norm_shift))


def up_kernel(core_ref, act_ref, own_ref, other_ref, bias_ref, out_ref, wnat_ref, *, width_cols):
    chips, slab, _ = own_ref.shape
    channels = act_ref.shape[1]
    core = core_ref[0]
    for z in range(chips):
        mine = pl.multiple_of(2 * slab * z + slab * core, slab)
        theirs = pl.multiple_of(2 * slab * z + slab * (1 - core), slab)
        wnat_ref[pl.ds(mine, slab), :] = own_ref[z, :, pl.ds(0, 4 * channels)]
        wnat_ref[pl.ds(theirs, slab), :] = other_ref[z, :, pl.ds(0, 4 * channels)]
    act = act_ref[...]
    rows = out_ref.shape[0]
    outs = wnat_ref.shape[0]
    for ab in range(4):
        a, b = divmod(ab, 2)
        res = lax.dot_general(act, wnat_ref[:, pl.ds(ab * channels, channels)], (((1,), (1,)), ((), ())),
                              preferred_element_type=jnp.float32)
        res = (res + bias_ref[...]).astype(out_ref.dtype)
        for i in range(rows):
            out_ref[i, a, :, pl.ds(b * outs, outs)] = res[i * width_cols:(i + 1) * width_cols, :]


def up_conv(core, act, own, other, bias_row):
    rows, width_cols, channels = act.shape
    chips, slab, _ = own.shape
    outs = 2 * chips * slab
    vmem = pl.BlockSpec(memory_space=pltpu.VMEM)
    smem = pl.BlockSpec(memory_space=pltpu.SMEM)
    return pl.pallas_call(
        functools.partial(up_kernel, width_cols=width_cols),
        out_shape=jax.ShapeDtypeStruct((rows, 2, width_cols, 2 * outs), jnp.bfloat16),
        in_specs=[smem, vmem, vmem, vmem, vmem],
        out_specs=vmem,
        scratch_shapes=[pltpu.VMEM((outs, 4 * channels), jnp.bfloat16)],
        cost_estimate=pl.CostEstimate(
            flops=2 * rows * width_cols * channels * 4 * outs, transcendentals=0,
            bytes_accessed=act.size * 2 + 2 * own.size * 2 + rows * width_cols * 4 * outs * 2),
    )(jnp.reshape(core, (1,)).astype(jnp.int32), act.reshape(rows * width_cols, channels), own, other, bias_row)


def ring_gather(block, axis):
    chips = lax.axis_size(axis)
    step_up = [(i, (i - 1) % chips) for i in range(chips)]
    step_down = [(i, (i + 1) % chips) for i in range(chips)]
    ahead, behind = block, block
    from_ahead, from_behind = [], []
    for k in range(1, chips // 2 + 1):
        ahead = lax.ppermute(ahead, axis, step_up)
        from_ahead.append(ahead)
        if k < chips - chips // 2:
            behind = lax.ppermute(behind, axis, step_down)
            from_behind.append(behind)
    stacked = jnp.stack([block] + from_ahead + from_behind[::-1])
    return jnp.roll(stacked, lax.axis_index(axis), axis=0)


def body(coarse, conv_weight, conv_bias, norm_gain, norm_shift, up_weight, up_bias):
    chips = lax.axis_size("z")
    core = lax.axis_index("core")
    _, width_cols, channels = coarse.shape
    outputs = conv_weight.shape[0]
    slice_out = up_weight.shape[0]

    whole = lax.all_gather(coarse, ("z", "core"), axis=0, tiled=True)
    height = whole.shape[0]
    flat = up_weight.reshape(slice_out, -1)
    packed = jnp.concatenate([flat, jnp.pad(up_bias[:, None], ((0, 0), (0, 127)))], axis=1)
    packed_z = ring_gather(packed, "z")
    packed_other = lax.ppermute(packed_z, "core", [(0, 1), (1, 0)])
    bias_halves = jnp.stack([packed_z[:, :, flat.shape[1]], packed_other[:, :, flat.shape[1]]], axis=1)
    bias_halves = jnp.where(core == 0, bias_halves, bias_halves[:, ::-1])
    bias_row = bias_halves.astype(jnp.float32).reshape(1, -1)

    activated = conv_norm(whole, conv_weight, conv_bias, norm_gain, norm_shift)
    activated = jnp.transpose(activated).reshape(height, width_cols, outputs)

    chip_rows = lax.all_to_all(activated, "z", split_axis=0, concat_axis=2, tiled=True)
    both = lax.all_gather(chip_rows, "core", axis=0, tiled=False)
    half = chip_rows.shape[0] // 2
    own = lax.dynamic_slice_in_dim(both, core * half, half, axis=1)
    own = own.reshape((2, half, width_cols, chips, outputs))
    own = jnp.transpose(own, (1, 2, 3, 0, 4)).reshape(half, width_cols, channels)

    fine = up_conv(core, own, packed_z, packed_other, bias_row)
    return fine.reshape(2 * half, 2 * width_cols, -1)


def solution(mesh):
    grp, sp = mesh.devices.shape
    fine_mesh = Mesh(mesh.devices.reshape(grp, sp // 2, 2), ("grp", "z", "core"))
    rows = ("grp", "z", "core")
    chans = ("z", "core")
    return jax.shard_map(
        body,
        mesh=fine_mesh,
        in_specs=(
            P(rows, None, None),
            P(chans, None, None, None),
            P(chans),
            P(chans),
            P(chans),
            P(chans, None, None, None),
            P(chans),
        ),
        out_specs=P(rows, None, None),
        check_vma=False,
    )
```

```python
import functools

import jax
import jax.numpy as jnp
from jax import lax
from jax.experimental import pallas as pl
from jax.experimental.pallas import tpu as pltpu
from jax.sharding import Mesh, PartitionSpec as P

GSIZE = 32


def conv_norm_kernel(x_ref, w_ref, bias_ref, gain_ref, shift_ref, out_ref, *, height, width_cols):
    outputs = out_ref.shape[0]
    positions = height * width_cols
    taps = lax.dot_general(w_ref[...], x_ref[...], (((1,), (1,)), ((), ())),
                           preferred_element_type=jnp.float32)
    pos = lax.broadcasted_iota(jnp.int32, (1, positions), 1)
    row = pos // width_cols
    col = pos % width_cols
    acc = jnp.zeros((outputs, positions), jnp.float32)
    for t in range(9):
        r, s = divmod(t, 3)
        off = (r - 1) * width_cols + (s - 1)
        part = taps[t * outputs:(t + 1) * outputs, :]
        if off:
            part = pltpu.roll(part, (-off) % positions, 1)
        valid = ((row + (r - 1) >= 0) & (row + (r - 1) < height)
                 & (col + (s - 1) >= 0) & (col + (s - 1) < width_cols))
        acc = acc + jnp.where(valid, part, 0.0)
    conv = acc + bias_ref[...]
    groups = outputs // GSIZE
    grouped = conv.reshape(groups, GSIZE, positions)
    count = GSIZE * positions
    centre = jnp.sum(jnp.sum(grouped, axis=2, keepdims=True), axis=1, keepdims=True) / count
    dev = grouped - centre
    spread = jnp.sum(jnp.sum(dev * dev, axis=2, keepdims=True), axis=1, keepdims=True) / count
    normed = (dev * lax.rsqrt(spread + 1e-05)).reshape(outputs, positions)
    v = normed * gain_ref[...] + shift_ref[...]
    out_ref[...] = (v / (1.0 + jnp.exp(-v))).astype(out_ref.dtype)


def conv_norm(whole, conv_weight, conv_bias, norm_gain, norm_shift):
    height, width_cols, channels = whole.shape
    outputs = conv_weight.shape[0]
    x = whole.reshape(height * width_cols, channels)
    w = jnp.transpose(conv_weight.reshape(outputs, 9, channels), (1, 0, 2)).reshape(9 * outputs, channels)
    col = lambda v: v.astype(jnp.float32).reshape(outputs, 1)
    vmem = pl.BlockSpec(memory_space=pltpu.VMEM)
    return pl.pallas_call(
        functools.partial(conv_norm_kernel, height=height, width_cols=width_cols),
        out_shape=jax.ShapeDtypeStruct((outputs, height * width_cols), jnp.bfloat16),
        in_specs=[vmem] * 5,
        out_specs=vmem,
        cost_estimate=pl.CostEstimate(
            flops=2 * height * width_cols * channels * 9 * outputs,
            transcendentals=height * width_cols * outputs,
            bytes_accessed=x.size * 2 + w.size * 2 + outputs * height * width_cols * 2),
    )(x, w, col(conv_bias), col(norm_gain), col(norm_shift))


def up_kernel(index_ref, act_ref, own_ref, other_ref, out_ref, wnat_ref, *, width_cols):
    chips, slab, packed_width = own_ref.shape
    positions, channels = act_ref.shape
    core = index_ref[0]
    here = index_ref[1]
    for m in range(chips):
        chip = (here + m) % chips
        mine = pl.multiple_of(2 * slab * chip + slab * core, slab)
        theirs = pl.multiple_of(2 * slab * chip + slab * (1 - core), slab)
        wnat_ref[pl.ds(mine, slab), :] = own_ref[m]
        wnat_ref[pl.ds(theirs, slab), :] = other_ref[m]
    act = act_ref[...]
    rows = out_ref.shape[0]
    outs = wnat_ref.shape[0]
    nt = (((1,), (1,)), ((), ()))
    lane = lax.broadcasted_iota(jnp.int32, (positions, packed_width - 4 * channels), 1)
    ones = jnp.where(lane == 0, 1.0, 0.0).astype(act.dtype)
    bias = lax.dot_general(ones, wnat_ref[:, pl.ds(4 * channels, packed_width - 4 * channels)], nt,
                           preferred_element_type=jnp.float32)
    for ab in range(4):
        a, b = divmod(ab, 2)
        res = lax.dot_general(act, wnat_ref[:, pl.ds(ab * channels, channels)], nt,
                              preferred_element_type=jnp.float32)
        res = (res + bias).astype(out_ref.dtype)
        for i in range(rows):
            out_ref[i, a, :, pl.ds(b * outs, outs)] = res[i * width_cols:(i + 1) * width_cols, :]


def up_conv(core, here, act, own, other):
    rows, width_cols, channels = act.shape
    chips, slab, packed_width = own.shape
    outs = 2 * chips * slab
    vmem = pl.BlockSpec(memory_space=pltpu.VMEM)
    smem = pl.BlockSpec(memory_space=pltpu.SMEM)
    index = jnp.stack([core, here]).astype(jnp.int32)
    return pl.pallas_call(
        functools.partial(up_kernel, width_cols=width_cols),
        out_shape=jax.ShapeDtypeStruct((rows, 2, width_cols, 2 * outs), jnp.bfloat16),
        in_specs=[smem, vmem, vmem, vmem],
        out_specs=vmem,
        scratch_shapes=[pltpu.VMEM((outs, packed_width), jnp.bfloat16)],
        cost_estimate=pl.CostEstimate(
            flops=2 * rows * width_cols * channels * 4 * outs, transcendentals=0,
            bytes_accessed=act.size * 2 + 2 * own.size * 2 + rows * width_cols * 4 * outs * 2),
    )(index, act.reshape(rows * width_cols, channels), own, other)


def ring_gather(block, axis):
    chips = lax.axis_size(axis)
    step_up = [(i, (i - 1) % chips) for i in range(chips)]
    step_down = [(i, (i + 1) % chips) for i in range(chips)]
    ahead, behind = block, block
    from_ahead, from_behind = [], []
    for k in range(1, chips // 2 + 1):
        ahead = lax.ppermute(ahead, axis, step_up)
        from_ahead.append(ahead)
        if k < chips - chips // 2:
            behind = lax.ppermute(behind, axis, step_down)
            from_behind.append(behind)
    return jnp.stack([block] + from_ahead + from_behind[::-1])


def body(coarse, conv_weight, conv_bias, norm_gain, norm_shift, up_weight, up_bias):
    chips = lax.axis_size("z")
    core = lax.axis_index("core")
    _, width_cols, channels = coarse.shape
    outputs = conv_weight.shape[0]
    slice_out = up_weight.shape[0]

    whole = lax.all_gather(coarse, ("z", "core"), axis=0, tiled=True)
    height = whole.shape[0]
    flat = up_weight.reshape(slice_out, -1)
    packed = jnp.concatenate([flat, jnp.pad(up_bias[:, None], ((0, 0), (0, 127)))], axis=1)
    packed_z = ring_gather(packed, "z")
    packed_other = lax.ppermute(packed_z, "core", [(0, 1), (1, 0)])

    activated = conv_norm(whole, conv_weight, conv_bias, norm_gain, norm_shift)
    activated = jnp.transpose(activated).reshape(height, width_cols, outputs)

    chip_rows = lax.all_to_all(activated, "z", split_axis=0, concat_axis=2, tiled=True)
    both = lax.all_gather(chip_rows, "core", axis=0, tiled=False)
    half = chip_rows.shape[0] // 2
    own = lax.dynamic_slice_in_dim(both, core * half, half, axis=1)
    own = own.reshape((2, half, width_cols, chips, outputs))
    own = jnp.transpose(own, (1, 2, 3, 0, 4)).reshape(half, width_cols, channels)

    fine = up_conv(core, lax.axis_index("z"), own, packed_z, packed_other)
    return fine.reshape(2 * half, 2 * width_cols, -1)


def solution(mesh):
    grp, sp = mesh.devices.shape
    fine_mesh = Mesh(mesh.devices.reshape(grp, sp // 2, 2), ("grp", "z", "core"))
    rows = ("grp", "z", "core")
    chans = ("z", "core")
    return jax.shard_map(
        body,
        mesh=fine_mesh,
        in_specs=(
            P(rows, None, None),
            P(chans, None, None, None),
            P(chans),
            P(chans),
            P(chans),
            P(chans, None, None, None),
            P(chans),
        ),
        out_specs=P(rows, None, None),
        check_vma=False,
    )
```

```python
import functools

import jax
import jax.numpy as jnp
from jax import lax
from jax.experimental import pallas as pl
from jax.experimental.pallas import tpu as pltpu
from jax.sharding import Mesh, PartitionSpec as P

GSIZE = 32


def conv_norm_kernel(x_ref, w_ref, bias_ref, gain_ref, shift_ref, out_ref, *, height, width_cols):
    outputs = out_ref.shape[0]
    positions = height * width_cols
    taps = lax.dot_general(w_ref[...], x_ref[...], (((1,), (1,)), ((), ())),
                           preferred_element_type=jnp.float32)
    pos = lax.broadcasted_iota(jnp.int32, (1, positions), 1)
    row = pos // width_cols
    col = pos % width_cols
    acc = jnp.zeros((outputs, positions), jnp.float32)
    for t in range(9):
        r, s = divmod(t, 3)
        off = (r - 1) * width_cols + (s - 1)
        part = taps[t * outputs:(t + 1) * outputs, :]
        if off:
            part = pltpu.roll(part, (-off) % positions, 1)
        valid = ((row + (r - 1) >= 0) & (row + (r - 1) < height)
                 & (col + (s - 1) >= 0) & (col + (s - 1) < width_cols))
        acc = acc + jnp.where(valid, part, 0.0)
    conv = acc + bias_ref[...]
    groups = outputs // GSIZE
    grouped = conv.reshape(groups, GSIZE, positions)
    count = GSIZE * positions
    centre = jnp.sum(jnp.sum(grouped, axis=2, keepdims=True), axis=1, keepdims=True) / count
    dev = grouped - centre
    spread = jnp.sum(jnp.sum(dev * dev, axis=2, keepdims=True), axis=1, keepdims=True) / count
    normed = (dev * lax.rsqrt(spread + 1e-05)).reshape(outputs, positions)
    v = normed * gain_ref[...] + shift_ref[...]
    out_ref[...] = (v / (1.0 + jnp.exp(-v))).astype(out_ref.dtype)


def conv_norm(whole, conv_weight, conv_bias, norm_gain, norm_shift):
    height, width_cols, channels = whole.shape
    outputs = conv_weight.shape[0]
    x = whole.reshape(height * width_cols, channels)
    w = jnp.transpose(conv_weight.reshape(outputs, 9, channels), (1, 0, 2)).reshape(9 * outputs, channels)
    col = lambda v: v.astype(jnp.float32).reshape(outputs, 1)
    vmem = pl.BlockSpec(memory_space=pltpu.VMEM)
    return pl.pallas_call(
        functools.partial(conv_norm_kernel, height=height, width_cols=width_cols),
        out_shape=jax.ShapeDtypeStruct((outputs, height * width_cols), jnp.bfloat16),
        in_specs=[vmem] * 5,
        out_specs=vmem,
        cost_estimate=pl.CostEstimate(
            flops=2 * height * width_cols * channels * 9 * outputs,
            transcendentals=height * width_cols * outputs,
            bytes_accessed=x.size * 2 + w.size * 2 + outputs * height * width_cols * 2),
    )(x, w, col(conv_bias), col(norm_gain), col(norm_shift))


def up_kernel(index_ref, act_ref, own_ref, other_ref, out_ref, wnat_ref, actn_ref, *, width_cols):
    chips, slab, packed_width = own_ref.shape
    channels, positions = act_ref.shape
    block = channels // (2 * chips)
    core = index_ref[0]
    here = index_ref[1]
    for m in range(chips):
        chip = (here + m) % chips
        mine = pl.multiple_of(2 * slab * chip + slab * core, slab)
        theirs = pl.multiple_of(2 * slab * chip + slab * (1 - core), slab)
        wnat_ref[pl.ds(mine, slab), :] = own_ref[m]
        wnat_ref[pl.ds(theirs, slab), :] = other_ref[m]
    for c in range(2):
        for z in range(chips):
            actn_ref[pl.ds((2 * z + c) * block, block), :] = act_ref[pl.ds((c * chips + z) * block, block), :]
    rows = out_ref.shape[0]
    outs = wnat_ref.shape[0]
    nn = (((1,), (0,)), ((), ()))
    sub = lax.broadcasted_iota(jnp.int32, (packed_width - 4 * channels, positions), 0)
    ones = jnp.where(sub == 0, 1.0, 0.0).astype(actn_ref.dtype)
    bias = lax.dot_general(wnat_ref[:, pl.ds(4 * channels, packed_width - 4 * channels)], ones, nn,
                           preferred_element_type=jnp.float32)
    act = actn_ref[...]
    for ab in range(4):
        a, b = divmod(ab, 2)
        res = lax.dot_general(wnat_ref[:, pl.ds(ab * channels, channels)], act, nn,
                              preferred_element_type=jnp.float32)
        res = jnp.transpose(res + bias).astype(out_ref.dtype)
        span = rows * width_cols
        res = jnp.where(core == 0, res[:span], res[span:])
        for i in range(rows):
            out_ref[i, a, :, pl.ds(b * outs, outs)] = res[i * width_cols:(i + 1) * width_cols, :]


def up_conv(core, here, act, own, other, rows):
    channels, positions = act.shape
    width_cols = positions // (2 * rows)
    chips, slab, packed_width = own.shape
    outs = 2 * chips * slab
    vmem = pl.BlockSpec(memory_space=pltpu.VMEM)
    smem = pl.BlockSpec(memory_space=pltpu.SMEM)
    index = jnp.stack([core, here]).astype(jnp.int32)
    return pl.pallas_call(
        functools.partial(up_kernel, width_cols=width_cols),
        out_shape=jax.ShapeDtypeStruct((rows, 2, width_cols, 2 * outs), jnp.bfloat16),
        in_specs=[smem, vmem, vmem, vmem],
        out_specs=vmem,
        scratch_shapes=[pltpu.VMEM((outs, packed_width), jnp.bfloat16), pltpu.VMEM((channels, positions), act.dtype)],
        cost_estimate=pl.CostEstimate(
            flops=2 * positions * channels * 4 * outs, transcendentals=0,
            bytes_accessed=act.size * 2 + 2 * own.size * 2 + rows * width_cols * 4 * outs * 2),
    )(index, act, own, other)


def ring_gather(block, axis):
    chips = lax.axis_size(axis)
    step_up = [(i, (i - 1) % chips) for i in range(chips)]
    step_down = [(i, (i + 1) % chips) for i in range(chips)]
    ahead, behind = block, block
    from_ahead, from_behind = [], []
    for k in range(1, chips // 2 + 1):
        ahead = lax.ppermute(ahead, axis, step_up)
        from_ahead.append(ahead)
        if k < chips - chips // 2:
            behind = lax.ppermute(behind, axis, step_down)
            from_behind.append(behind)
    return jnp.stack([block] + from_ahead + from_behind[::-1])


def body(coarse, conv_weight, conv_bias, norm_gain, norm_shift, up_weight, up_bias):
    chips = lax.axis_size("z")
    core = lax.axis_index("core")
    _, width_cols, channels = coarse.shape
    outputs = conv_weight.shape[0]
    slice_out = up_weight.shape[0]

    whole = lax.all_gather(coarse, ("z", "core"), axis=0, tiled=True)
    height = whole.shape[0]
    flat = up_weight.reshape(slice_out, -1)
    packed = jnp.concatenate([flat, jnp.pad(up_bias[:, None], ((0, 0), (0, 127)))], axis=1)
    packed_z = ring_gather(packed, "z")
    packed_other = lax.ppermute(packed_z, "core", [(0, 1), (1, 0)])

    activated = conv_norm(whole, conv_weight, conv_bias, norm_gain, norm_shift)
    chip_rows = lax.all_to_all(activated, "z", split_axis=1, concat_axis=0, tiled=True)
    both = lax.all_gather(chip_rows, "core", axis=0, tiled=True)
    half = coarse.shape[0]
    fine = up_conv(core, lax.axis_index("z"), both, packed_z, packed_other, half)
    return fine.reshape(2 * half, 2 * width_cols, -1)


def solution(mesh):
    grp, sp = mesh.devices.shape
    fine_mesh = Mesh(mesh.devices.reshape(grp, sp // 2, 2), ("grp", "z", "core"))
    rows = ("grp", "z", "core")
    chans = ("z", "core")
    return jax.shard_map(
        body,
        mesh=fine_mesh,
        in_specs=(
            P(rows, None, None),
            P(chans, None, None, None),
            P(chans),
            P(chans),
            P(chans),
            P(chans, None, None, None),
            P(chans),
        ),
        out_specs=P(rows, None, None),
        check_vma=False,
    )
```

```python
import functools

import jax
import jax.numpy as jnp
from jax import lax
from jax.experimental import pallas as pl
from jax.experimental.pallas import tpu as pltpu
from jax.sharding import Mesh, PartitionSpec as P

GSIZE = 32


def conv_norm_kernel(x_ref, w_ref, bias_ref, gain_ref, shift_ref, out_ref, *, height, width_cols):
    outputs = out_ref.shape[0]
    positions = height * width_cols
    taps = lax.dot_general(w_ref[...], x_ref[...], (((1,), (1,)), ((), ())),
                           preferred_element_type=jnp.float32)
    pos = lax.broadcasted_iota(jnp.int32, (1, positions), 1)
    row = pos // width_cols
    col = pos % width_cols
    acc = jnp.zeros((outputs, positions), jnp.float32)
    for t in range(9):
        r, s = divmod(t, 3)
        off = (r - 1) * width_cols + (s - 1)
        part = taps[t * outputs:(t + 1) * outputs, :]
        if off:
            part = pltpu.roll(part, (-off) % positions, 1)
        valid = ((row + (r - 1) >= 0) & (row + (r - 1) < height)
                 & (col + (s - 1) >= 0) & (col + (s - 1) < width_cols))
        acc = acc + jnp.where(valid, part, 0.0)
    conv = acc + bias_ref[...]
    groups = outputs // GSIZE
    grouped = conv.reshape(groups, GSIZE, positions)
    count = GSIZE * positions
    centre = jnp.sum(jnp.sum(grouped, axis=2, keepdims=True), axis=1, keepdims=True) / count
    dev = grouped - centre
    spread = jnp.sum(jnp.sum(dev * dev, axis=2, keepdims=True), axis=1, keepdims=True) / count
    normed = (dev * lax.rsqrt(spread + 1e-05)).reshape(outputs, positions)
    v = normed * gain_ref[...] + shift_ref[...]
    out_ref[...] = (v / (1.0 + jnp.exp(-v))).astype(out_ref.dtype)


def conv_norm(whole, conv_weight, conv_bias, norm_gain, norm_shift):
    height, width_cols, channels = whole.shape
    outputs = conv_weight.shape[0]
    x = whole.reshape(height * width_cols, channels)
    w = jnp.transpose(conv_weight.reshape(outputs, 9, channels), (1, 0, 2)).reshape(9 * outputs, channels)
    col = lambda v: v.astype(jnp.float32).reshape(outputs, 1)
    vmem = pl.BlockSpec(memory_space=pltpu.VMEM)
    return pl.pallas_call(
        functools.partial(conv_norm_kernel, height=height, width_cols=width_cols),
        out_shape=jax.ShapeDtypeStruct((outputs, height * width_cols), jnp.bfloat16),
        in_specs=[vmem] * 5,
        out_specs=vmem,
        cost_estimate=pl.CostEstimate(
            flops=2 * height * width_cols * channels * 9 * outputs,
            transcendentals=height * width_cols * outputs,
            bytes_accessed=x.size * 2 + w.size * 2 + outputs * height * width_cols * 2),
    )(x, w, col(conv_bias), col(norm_gain), col(norm_shift))


def up_kernel(index_ref, act_ref, own_ref, other_ref, out_ref, wnat_ref, actn_ref, *, width_cols):
    chips, slab, packed_width = own_ref.shape
    channels, positions = act_ref.shape
    block = channels // (2 * chips)
    core = index_ref[0]
    here = index_ref[1]
    for m in range(chips):
        chip = (here + m) % chips
        mine = pl.multiple_of(2 * slab * chip + slab * core, slab)
        theirs = pl.multiple_of(2 * slab * chip + slab * (1 - core), slab)
        wnat_ref[pl.ds(mine, slab), :] = own_ref[m]
        wnat_ref[pl.ds(theirs, slab), :] = other_ref[m]
    for c in range(2):
        for z in range(chips):
            actn_ref[pl.ds((2 * z + c) * block, block), :] = act_ref[pl.ds((c * chips + z) * block, block), :]
    rows = out_ref.shape[0] // 2
    outs = wnat_ref.shape[0]
    nn = (((1,), (0,)), ((), ()))
    sub = lax.broadcasted_iota(jnp.int32, (packed_width - 4 * channels, positions), 0)
    ones = jnp.where(sub == 0, 1.0, 0.0).astype(actn_ref.dtype)
    bias = lax.dot_general(wnat_ref[:, pl.ds(4 * channels, packed_width - 4 * channels)], ones, nn,
                           preferred_element_type=jnp.float32)
    act = actn_ref[...]
    span = rows * width_cols
    dest = lax.broadcasted_iota(jnp.int32, (2 * width_cols, 2 * width_cols), 0)
    src = lax.broadcasted_iota(jnp.int32, (2 * width_cols, 2 * width_cols), 1)
    interleave = jnp.where(src == (dest % 2) * width_cols + dest // 2, 1.0, 0.0).astype(out_ref.dtype)
    for a in range(2):
        phases = []
        for b in range(2):
            res = lax.dot_general(wnat_ref[:, pl.ds((2 * a + b) * channels, channels)], act, nn,
                                  preferred_element_type=jnp.float32)
            res = jnp.transpose(res + bias).astype(out_ref.dtype)
            phases.append(jnp.where(core == 0, res[:span], res[span:]))
        for i in range(rows):
            stacked = jnp.concatenate([p[i * width_cols:(i + 1) * width_cols] for p in phases], axis=0)
            out_ref[2 * i + a] = jnp.dot(interleave, stacked, preferred_element_type=jnp.float32).astype(out_ref.dtype)


def up_conv(core, here, act, own, other, rows):
    channels, positions = act.shape
    width_cols = positions // (2 * rows)
    chips, slab, packed_width = own.shape
    outs = 2 * chips * slab
    vmem = pl.BlockSpec(memory_space=pltpu.VMEM)
    smem = pl.BlockSpec(memory_space=pltpu.SMEM)
    index = jnp.stack([core, here]).astype(jnp.int32)
    return pl.pallas_call(
        functools.partial(up_kernel, width_cols=width_cols),
        out_shape=jax.ShapeDtypeStruct((2 * rows, 2 * width_cols, outs), jnp.bfloat16),
        in_specs=[smem, vmem, vmem, vmem],
        out_specs=vmem,
        scratch_shapes=[pltpu.VMEM((outs, packed_width), jnp.bfloat16), pltpu.VMEM((channels, positions), act.dtype)],
        cost_estimate=pl.CostEstimate(
            flops=2 * positions * channels * 4 * outs, transcendentals=0,
            bytes_accessed=act.size * 2 + 2 * own.size * 2 + rows * width_cols * 4 * outs * 2),
    )(index, act, own, other)


def ring_gather(block, axis):
    chips = lax.axis_size(axis)
    step_up = [(i, (i - 1) % chips) for i in range(chips)]
    step_down = [(i, (i + 1) % chips) for i in range(chips)]
    ahead, behind = block, block
    from_ahead, from_behind = [], []
    for k in range(1, chips // 2 + 1):
        ahead = lax.ppermute(ahead, axis, step_up)
        from_ahead.append(ahead)
        if k < chips - chips // 2:
            behind = lax.ppermute(behind, axis, step_down)
            from_behind.append(behind)
    return jnp.stack([block] + from_ahead + from_behind[::-1])


def body(coarse, conv_weight, conv_bias, norm_gain, norm_shift, up_weight, up_bias):
    chips = lax.axis_size("z")
    core = lax.axis_index("core")
    _, width_cols, channels = coarse.shape
    outputs = conv_weight.shape[0]
    slice_out = up_weight.shape[0]

    whole = lax.all_gather(coarse, ("z", "core"), axis=0, tiled=True)
    height = whole.shape[0]
    flat = up_weight.reshape(slice_out, -1)
    packed = jnp.concatenate([flat, jnp.pad(up_bias[:, None], ((0, 0), (0, 127)))], axis=1)
    packed_z = ring_gather(packed, "z")
    packed_other = lax.ppermute(packed_z, "core", [(0, 1), (1, 0)])

    activated = conv_norm(whole, conv_weight, conv_bias, norm_gain, norm_shift)
    chip_rows = lax.all_to_all(activated, "z", split_axis=1, concat_axis=0, tiled=True)
    both = lax.all_gather(chip_rows, "core", axis=0, tiled=True)
    half = coarse.shape[0]
    fine = up_conv(core, lax.axis_index("z"), both, packed_z, packed_other, half)
    return fine.reshape(2 * half, 2 * width_cols, -1)


def solution(mesh):
    grp, sp = mesh.devices.shape
    fine_mesh = Mesh(mesh.devices.reshape(grp, sp // 2, 2), ("grp", "z", "core"))
    rows = ("grp", "z", "core")
    chans = ("z", "core")
    return jax.shard_map(
        body,
        mesh=fine_mesh,
        in_specs=(
            P(rows, None, None),
            P(chans, None, None, None),
            P(chans),
            P(chans),
            P(chans),
            P(chans, None, None, None),
            P(chans),
        ),
        out_specs=P(rows, None, None),
        check_vma=False,
    )
```

```python
import functools

import jax
import jax.numpy as jnp
from jax import lax
from jax.experimental import pallas as pl
from jax.experimental.pallas import tpu as pltpu
from jax.sharding import Mesh, PartitionSpec as P

GSIZE = 32


def conv_norm_kernel(x_ref, w_ref, bias_ref, gain_ref, shift_ref, out_ref, taps_ref, *, height, width_cols):
    outputs = out_ref.shape[0]
    positions = height * width_cols
    chunk = x_ref.shape[0]
    step = pl.program_id(0)
    at = pl.multiple_of(step * chunk, 128)
    taps_ref[:, pl.ds(at, chunk)] = lax.dot_general(w_ref[...], x_ref[...], (((1,), (1,)), ((), ())),
                                                   preferred_element_type=jnp.float32)

    @pl.when(step == pl.num_programs(0) - 1)
    def _():
        taps = taps_ref[...]
        pos = lax.broadcasted_iota(jnp.int32, (1, positions), 1)
        row = pos // width_cols
        col = pos % width_cols
        acc = jnp.zeros((outputs, positions), jnp.float32)
        for t in range(9):
            r, s = divmod(t, 3)
            off = (r - 1) * width_cols + (s - 1)
            part = taps[t * outputs:(t + 1) * outputs, :]
            if off:
                part = pltpu.roll(part, (-off) % positions, 1)
            valid = ((row + (r - 1) >= 0) & (row + (r - 1) < height)
                     & (col + (s - 1) >= 0) & (col + (s - 1) < width_cols))
            acc = acc + jnp.where(valid, part, 0.0)
        conv = acc + bias_ref[...]
        groups = outputs // GSIZE
        grouped = conv.reshape(groups, GSIZE, positions)
        count = GSIZE * positions
        centre = jnp.sum(jnp.sum(grouped, axis=2, keepdims=True), axis=1, keepdims=True) / count
        dev = grouped - centre
        spread = jnp.sum(jnp.sum(dev * dev, axis=2, keepdims=True), axis=1, keepdims=True) / count
        normed = (dev * lax.rsqrt(spread + 1e-05)).reshape(outputs, positions)
        v = normed * gain_ref[...] + shift_ref[...]
        out_ref[...] = (v / (1.0 + jnp.exp(-v))).astype(out_ref.dtype)


def conv_norm(whole, conv_weight, conv_bias, norm_gain, norm_shift):
    height, width_cols, channels = whole.shape
    outputs = conv_weight.shape[0]
    positions = height * width_cols
    chunk = positions // 4
    x = whole.reshape(positions, channels)
    w = jnp.transpose(conv_weight.reshape(outputs, 9, channels), (1, 0, 2)).reshape(9 * outputs, channels)
    col = lambda v: v.astype(jnp.float32).reshape(outputs, 1)
    fixed = lambda shape: pl.BlockSpec(shape, lambda i: (0, 0))
    return pl.pallas_call(
        functools.partial(conv_norm_kernel, height=height, width_cols=width_cols),
        out_shape=jax.ShapeDtypeStruct((outputs, positions), jnp.bfloat16),
        grid=(positions // chunk,),
        in_specs=[pl.BlockSpec((chunk, channels), lambda i: (i, 0)), fixed((9 * outputs, channels)),
                  fixed((outputs, 1)), fixed((outputs, 1)), fixed((outputs, 1))],
        out_specs=fixed((outputs, positions)),
        scratch_shapes=[pltpu.VMEM((9 * outputs, positions), jnp.float32)],
        cost_estimate=pl.CostEstimate(
            flops=2 * positions * channels * 9 * outputs,
            transcendentals=positions * outputs,
            bytes_accessed=x.size * 2 + w.size * 2 + outputs * positions * 2),
    )(x, w, col(conv_bias), col(norm_gain), col(norm_shift))


def up_kernel(index_ref, act_ref, own_ref, other_ref, out_ref, wnat_ref, actn_ref, *, width_cols):
    chips, slab, packed_width = own_ref.shape
    channels, positions = act_ref.shape
    block = channels // (2 * chips)
    core = index_ref[0]
    here = index_ref[1]
    for m in range(chips):
        chip = (here + m) % chips
        mine = pl.multiple_of(2 * slab * chip + slab * core, slab)
        theirs = pl.multiple_of(2 * slab * chip + slab * (1 - core), slab)
        wnat_ref[pl.ds(mine, slab), :] = own_ref[m]
        wnat_ref[pl.ds(theirs, slab), :] = other_ref[m]
    for c in range(2):
        for z in range(chips):
            actn_ref[pl.ds((2 * z + c) * block, block), :] = act_ref[pl.ds((c * chips + z) * block, block), :]
    rows = out_ref.shape[0] // 2
    outs = wnat_ref.shape[0]
    nn = (((1,), (0,)), ((), ()))
    sub = lax.broadcasted_iota(jnp.int32, (packed_width - 4 * channels, positions), 0)
    ones = jnp.where(sub == 0, 1.0, 0.0).astype(actn_ref.dtype)
    bias = lax.dot_general(wnat_ref[:, pl.ds(4 * channels, packed_width - 4 * channels)], ones, nn,
                           preferred_element_type=jnp.float32)
    act = actn_ref[...]
    span = rows * width_cols
    dest = lax.broadcasted_iota(jnp.int32, (2 * width_cols, 2 * width_cols), 0)
    src = lax.broadcasted_iota(jnp.int32, (2 * width_cols, 2 * width_cols), 1)
    interleave = jnp.where(src == (dest % 2) * width_cols + dest // 2, 1.0, 0.0).astype(out_ref.dtype)
    for a in range(2):
        phases = []
        for b in range(2):
            res = lax.dot_general(wnat_ref[:, pl.ds((2 * a + b) * channels, channels)], act, nn,
                                  preferred_element_type=jnp.float32)
            res = jnp.transpose(res + bias).astype(out_ref.dtype)
            phases.append(jnp.where(core == 0, res[:span], res[span:]))
        for i in range(rows):
            stacked = jnp.concatenate([p[i * width_cols:(i + 1) * width_cols] for p in phases], axis=0)
            out_ref[2 * i + a] = jnp.dot(interleave, stacked, preferred_element_type=jnp.float32).astype(out_ref.dtype)


def up_conv(core, here, act, own, other, rows):
    channels, positions = act.shape
    width_cols = positions // (2 * rows)
    chips, slab, packed_width = own.shape
    outs = 2 * chips * slab
    vmem = pl.BlockSpec(memory_space=pltpu.VMEM)
    smem = pl.BlockSpec(memory_space=pltpu.SMEM)
    index = jnp.stack([core, here]).astype(jnp.int32)
    return pl.pallas_call(
        functools.partial(up_kernel, width_cols=width_cols),
        out_shape=jax.ShapeDtypeStruct((2 * rows, 2 * width_cols, outs), jnp.bfloat16),
        in_specs=[smem, vmem, vmem, vmem],
        out_specs=vmem,
        scratch_shapes=[pltpu.VMEM((outs, packed_width), jnp.bfloat16), pltpu.VMEM((channels, positions), act.dtype)],
        cost_estimate=pl.CostEstimate(
            flops=2 * positions * channels * 4 * outs, transcendentals=0,
            bytes_accessed=act.size * 2 + 2 * own.size * 2 + rows * width_cols * 4 * outs * 2),
    )(index, act, own, other)


def ring_gather(block, axis):
    chips = lax.axis_size(axis)
    step_up = [(i, (i - 1) % chips) for i in range(chips)]
    step_down = [(i, (i + 1) % chips) for i in range(chips)]
    ahead, behind = block, block
    from_ahead, from_behind = [], []
    for k in range(1, chips // 2 + 1):
        ahead = lax.ppermute(ahead, axis, step_up)
        from_ahead.append(ahead)
        if k < chips - chips // 2:
            behind = lax.ppermute(behind, axis, step_down)
            from_behind.append(behind)
    return jnp.stack([block] + from_ahead + from_behind[::-1])


def body(coarse, conv_weight, conv_bias, norm_gain, norm_shift, up_weight, up_bias):
    chips = lax.axis_size("z")
    core = lax.axis_index("core")
    _, width_cols, channels = coarse.shape
    outputs = conv_weight.shape[0]
    slice_out = up_weight.shape[0]

    whole = lax.all_gather(coarse, ("z", "core"), axis=0, tiled=True)
    height = whole.shape[0]
    flat = up_weight.reshape(slice_out, -1)
    packed = jnp.concatenate([flat, jnp.pad(up_bias[:, None], ((0, 0), (0, 127)))], axis=1)
    packed_z = ring_gather(packed, "z")
    packed_other = lax.ppermute(packed_z, "core", [(0, 1), (1, 0)])

    activated = conv_norm(whole, conv_weight, conv_bias, norm_gain, norm_shift)
    chip_rows = lax.all_to_all(activated, "z", split_axis=1, concat_axis=0, tiled=True)
    both = lax.all_gather(chip_rows, "core", axis=0, tiled=True)
    half = coarse.shape[0]
    fine = up_conv(core, lax.axis_index("z"), both, packed_z, packed_other, half)
    return fine.reshape(2 * half, 2 * width_cols, -1)


def solution(mesh):
    grp, sp = mesh.devices.shape
    fine_mesh = Mesh(mesh.devices.reshape(grp, sp // 2, 2), ("grp", "z", "core"))
    rows = ("grp", "z", "core")
    chans = ("z", "core")
    return jax.shard_map(
        body,
        mesh=fine_mesh,
        in_specs=(
            P(rows, None, None),
            P(chans, None, None, None),
            P(chans),
            P(chans),
            P(chans),
            P(chans, None, None, None),
            P(chans),
        ),
        out_specs=P(rows, None, None),
        check_vma=False,
    )
```

```python
import functools

import jax
import jax.numpy as jnp
from jax import lax
from jax.experimental import pallas as pl
from jax.experimental.pallas import tpu as pltpu
from jax.sharding import Mesh, PartitionSpec as P

GSIZE = 32


def conv_norm_kernel(x_ref, w_ref, bias_ref, gain_ref, shift_ref, out_ref, *, height, width_cols):
    outputs = out_ref.shape[0]
    positions = height * width_cols
    taps = lax.dot_general(w_ref[...], x_ref[...], (((1,), (1,)), ((), ())),
                           preferred_element_type=jnp.float32)
    pos = lax.broadcasted_iota(jnp.int32, (1, positions), 1)
    row = pos // width_cols
    col = pos % width_cols
    acc = jnp.zeros((outputs, positions), jnp.float32)
    for t in range(9):
        r, s = divmod(t, 3)
        off = (r - 1) * width_cols + (s - 1)
        part = taps[t * outputs:(t + 1) * outputs, :]
        if off:
            part = pltpu.roll(part, (-off) % positions, 1)
        valid = ((row + (r - 1) >= 0) & (row + (r - 1) < height)
                 & (col + (s - 1) >= 0) & (col + (s - 1) < width_cols))
        acc = acc + jnp.where(valid, part, 0.0)
    conv = acc + bias_ref[...]
    groups = outputs // GSIZE
    grouped = conv.reshape(groups, GSIZE, positions)
    count = GSIZE * positions
    centre = jnp.sum(jnp.sum(grouped, axis=2, keepdims=True), axis=1, keepdims=True) / count
    dev = grouped - centre
    spread = jnp.sum(jnp.sum(dev * dev, axis=2, keepdims=True), axis=1, keepdims=True) / count
    normed = (dev * lax.rsqrt(spread + 1e-05)).reshape(outputs, positions)
    v = normed * gain_ref[...] + shift_ref[...]
    out_ref[...] = (v / (1.0 + jnp.exp(-v))).astype(out_ref.dtype)


def conv_norm(whole, conv_weight, conv_bias, norm_gain, norm_shift):
    height, width_cols, channels = whole.shape
    outputs = conv_weight.shape[0]
    x = whole.reshape(height * width_cols, channels)
    w = jnp.transpose(conv_weight.reshape(outputs, 9, channels), (1, 0, 2)).reshape(9 * outputs, channels)
    col = lambda v: v.astype(jnp.float32).reshape(outputs, 1)
    vmem = pl.BlockSpec(memory_space=pltpu.VMEM)
    return pl.pallas_call(
        functools.partial(conv_norm_kernel, height=height, width_cols=width_cols),
        out_shape=jax.ShapeDtypeStruct((outputs, height * width_cols), jnp.bfloat16),
        in_specs=[vmem] * 5,
        out_specs=vmem,
        cost_estimate=pl.CostEstimate(
            flops=2 * height * width_cols * channels * 9 * outputs,
            transcendentals=height * width_cols * outputs,
            bytes_accessed=x.size * 2 + w.size * 2 + outputs * height * width_cols * 2),
    )(x, w, col(conv_bias), col(norm_gain), col(norm_shift))


def up_kernel(index_ref, act_ref, own_ref, other_ref, out_ref, wnat_ref, *, width_cols):
    chips, slab, packed_width = own_ref.shape
    channels, positions = act_ref.shape
    core = index_ref[0]
    here = index_ref[1]
    for m in range(chips):
        chip = (here + m) % chips
        mine = pl.multiple_of(2 * slab * chip + slab * core, slab)
        theirs = pl.multiple_of(2 * slab * chip + slab * (1 - core), slab)
        wnat_ref[pl.ds(mine, slab), :] = own_ref[m]
        wnat_ref[pl.ds(theirs, slab), :] = other_ref[m]
    rows = out_ref.shape[0] // 2
    outs = wnat_ref.shape[0]
    nn = (((1,), (0,)), ((), ()))
    sub = lax.broadcasted_iota(jnp.int32, (packed_width - 4 * channels, positions), 0)
    ones = jnp.where(sub == 0, 1.0, 0.0).astype(act_ref.dtype)
    bias = lax.dot_general(wnat_ref[:, pl.ds(4 * channels, packed_width - 4 * channels)], ones, nn,
                           preferred_element_type=jnp.float32)
    act = act_ref[...]
    dest = lax.broadcasted_iota(jnp.int32, (2 * width_cols, 2 * width_cols), 0)
    src = lax.broadcasted_iota(jnp.int32, (2 * width_cols, 2 * width_cols), 1)
    interleave = jnp.where(src == (dest % 2) * width_cols + dest // 2, 1.0, 0.0).astype(out_ref.dtype)
    for a in range(2):
        phases = []
        for b in range(2):
            res = lax.dot_general(wnat_ref[:, pl.ds((2 * a + b) * channels, channels)], act, nn,
                                  preferred_element_type=jnp.float32)
            res = jnp.transpose(res + bias).astype(out_ref.dtype)
            phases.append(res)
        for i in range(rows):
            stacked = jnp.concatenate([p[i * width_cols:(i + 1) * width_cols] for p in phases], axis=0)
            out_ref[2 * i + a] = jnp.dot(interleave, stacked, preferred_element_type=jnp.float32).astype(out_ref.dtype)


def up_conv(core, here, act, own, other, rows):
    channels, positions = act.shape
    width_cols = positions // rows
    chips, slab, packed_width = own.shape
    outs = 2 * chips * slab
    vmem = pl.BlockSpec(memory_space=pltpu.VMEM)
    smem = pl.BlockSpec(memory_space=pltpu.SMEM)
    index = jnp.stack([core, here]).astype(jnp.int32)
    return pl.pallas_call(
        functools.partial(up_kernel, width_cols=width_cols),
        out_shape=jax.ShapeDtypeStruct((2 * rows, 2 * width_cols, outs), jnp.bfloat16),
        in_specs=[smem, vmem, vmem, vmem],
        out_specs=vmem,
        scratch_shapes=[pltpu.VMEM((outs, packed_width), jnp.bfloat16)],
        cost_estimate=pl.CostEstimate(
            flops=2 * positions * channels * 4 * outs, transcendentals=0,
            bytes_accessed=act.size * 2 + 2 * own.size * 2 + rows * width_cols * 4 * outs * 2),
    )(index, act, own, other)


def ring_gather(block, axis):
    chips = lax.axis_size(axis)
    step_up = [(i, (i - 1) % chips) for i in range(chips)]
    step_down = [(i, (i + 1) % chips) for i in range(chips)]
    ahead, behind = block, block
    from_ahead, from_behind = [], []
    for k in range(1, chips // 2 + 1):
        ahead = lax.ppermute(ahead, axis, step_up)
        from_ahead.append(ahead)
        if k < chips - chips // 2:
            behind = lax.ppermute(behind, axis, step_down)
            from_behind.append(behind)
    return jnp.stack([block] + from_ahead + from_behind[::-1])


def body(coarse, conv_weight, conv_bias, norm_gain, norm_shift, up_weight, up_bias):
    chips = lax.axis_size("z")
    core = lax.axis_index("core")
    _, width_cols, channels = coarse.shape
    outputs = conv_weight.shape[0]
    slice_out = up_weight.shape[0]

    whole = lax.all_gather(coarse, ("z", "core"), axis=0, tiled=True)
    height = whole.shape[0]
    flat = up_weight.reshape(slice_out, -1)
    packed = jnp.concatenate([flat, jnp.pad(up_bias[:, None], ((0, 0), (0, 127)))], axis=1)
    packed_z = ring_gather(packed, "z")
    packed_other = lax.ppermute(packed_z, "core", [(0, 1), (1, 0)])

    activated = conv_norm(whole, conv_weight, conv_bias, norm_gain, norm_shift)
    own_rows = lax.all_to_all(activated, ("z", "core"), split_axis=1, concat_axis=0, tiled=True)
    half = coarse.shape[0]
    fine = up_conv(core, lax.axis_index("z"), own_rows, packed_z, packed_other, half)
    return fine.reshape(2 * half, 2 * width_cols, -1)


def solution(mesh):
    grp, sp = mesh.devices.shape
    fine_mesh = Mesh(mesh.devices.reshape(grp, sp // 2, 2), ("grp", "z", "core"))
    rows = ("grp", "z", "core")
    chans = ("z", "core")
    return jax.shard_map(
        body,
        mesh=fine_mesh,
        in_specs=(
            P(rows, None, None),
            P(chans, None, None, None),
            P(chans),
            P(chans),
            P(chans),
            P(chans, None, None, None),
            P(chans),
        ),
        out_specs=P(rows, None, None),
        check_vma=False,
    )
```

```python
import functools

import jax
import jax.numpy as jnp
from jax import lax
from jax.experimental import pallas as pl
from jax.experimental.pallas import tpu as pltpu
from jax.sharding import Mesh, PartitionSpec as P

GSIZE = 32


def conv_norm_kernel(x_ref, w_ref, bias_ref, gain_ref, shift_ref, out_ref, *, height, width_cols):
    outputs = out_ref.shape[1]
    positions = height * width_cols
    taps = lax.dot_general(w_ref[...], x_ref[...], (((1,), (1,)), ((), ())),
                           preferred_element_type=jnp.float32)
    pos = lax.broadcasted_iota(jnp.int32, (1, positions), 1)
    row = pos // width_cols
    col = pos % width_cols
    acc = jnp.zeros((outputs, positions), jnp.float32)
    for t in range(9):
        r, s = divmod(t, 3)
        off = (r - 1) * width_cols + (s - 1)
        part = taps[t * outputs:(t + 1) * outputs, :]
        if off:
            part = pltpu.roll(part, (-off) % positions, 1)
        valid = ((row + (r - 1) >= 0) & (row + (r - 1) < height)
                 & (col + (s - 1) >= 0) & (col + (s - 1) < width_cols))
        acc = acc + jnp.where(valid, part, 0.0)
    conv = acc + bias_ref[...]
    groups = outputs // GSIZE
    grouped = conv.reshape(groups, GSIZE, positions)
    count = GSIZE * positions
    centre = jnp.sum(jnp.sum(grouped, axis=2, keepdims=True), axis=1, keepdims=True) / count
    dev = grouped - centre
    spread = jnp.sum(jnp.sum(dev * dev, axis=2, keepdims=True), axis=1, keepdims=True) / count
    normed = (dev * lax.rsqrt(spread + 1e-05)).reshape(outputs, positions)
    v = normed * gain_ref[...] + shift_ref[...]
    act = (v / (1.0 + jnp.exp(-v))).astype(out_ref.dtype)
    chips, _, span = out_ref.shape
    for chip in range(chips):
        out_ref[chip] = act[:, chip * span:(chip + 1) * span]


def conv_norm(whole, conv_weight, conv_bias, norm_gain, norm_shift, chips):
    height, width_cols, channels = whole.shape
    outputs = conv_weight.shape[0]
    x = whole.reshape(height * width_cols, channels)
    w = jnp.transpose(conv_weight.reshape(outputs, 9, channels), (1, 0, 2)).reshape(9 * outputs, channels)
    col = lambda v: v.astype(jnp.float32).reshape(outputs, 1)
    vmem = pl.BlockSpec(memory_space=pltpu.VMEM)
    return pl.pallas_call(
        functools.partial(conv_norm_kernel, height=height, width_cols=width_cols),
        out_shape=jax.ShapeDtypeStruct((chips, outputs, height * width_cols // chips), jnp.bfloat16),
        in_specs=[vmem] * 5,
        out_specs=vmem,
        cost_estimate=pl.CostEstimate(
            flops=2 * height * width_cols * channels * 9 * outputs,
            transcendentals=height * width_cols * outputs,
            bytes_accessed=x.size * 2 + w.size * 2 + outputs * height * width_cols * 2),
    )(x, w, col(conv_bias), col(norm_gain), col(norm_shift))


def up_kernel(index_ref, act_ref, own_ref, other_ref, out_ref, wnat_ref, actn_ref, *, width_cols):
    chips, slab, packed_width = own_ref.shape
    channels, positions = act_ref.shape
    block = channels // (2 * chips)
    core = index_ref[0]
    here = index_ref[1]
    for m in range(chips):
        chip = (here + m) % chips
        mine = pl.multiple_of(2 * slab * chip + slab * core, slab)
        theirs = pl.multiple_of(2 * slab * chip + slab * (1 - core), slab)
        wnat_ref[pl.ds(mine, slab), :] = own_ref[m]
        wnat_ref[pl.ds(theirs, slab), :] = other_ref[m]
    for c in range(2):
        for z in range(chips):
            actn_ref[pl.ds((2 * z + c) * block, block), :] = act_ref[pl.ds((c * chips + z) * block, block), :]
    rows = out_ref.shape[0] // 2
    outs = wnat_ref.shape[0]
    nn = (((1,), (0,)), ((), ()))
    sub = lax.broadcasted_iota(jnp.int32, (packed_width - 4 * channels, positions), 0)
    ones = jnp.where(sub == 0, 1.0, 0.0).astype(actn_ref.dtype)
    bias = lax.dot_general(wnat_ref[:, pl.ds(4 * channels, packed_width - 4 * channels)], ones, nn,
                           preferred_element_type=jnp.float32)
    act = actn_ref[...]
    span = rows * width_cols
    dest = lax.broadcasted_iota(jnp.int32, (2 * width_cols, 2 * width_cols), 0)
    src = lax.broadcasted_iota(jnp.int32, (2 * width_cols, 2 * width_cols), 1)
    interleave = jnp.where(src == (dest % 2) * width_cols + dest // 2, 1.0, 0.0).astype(out_ref.dtype)
    for a in range(2):
        phases = []
        for b in range(2):
            res = lax.dot_general(wnat_ref[:, pl.ds((2 * a + b) * channels, channels)], act, nn,
                                  preferred_element_type=jnp.float32)
            res = jnp.transpose(res + bias).astype(out_ref.dtype)
            phases.append(jnp.where(core == 0, res[:span], res[span:]))
        for i in range(rows):
            stacked = jnp.concatenate([p[i * width_cols:(i + 1) * width_cols] for p in phases], axis=0)
            out_ref[2 * i + a] = jnp.dot(interleave, stacked, preferred_element_type=jnp.float32).astype(out_ref.dtype)


def up_conv(core, here, act, own, other, rows):
    channels, positions = act.shape
    width_cols = positions // (2 * rows)
    chips, slab, packed_width = own.shape
    outs = 2 * chips * slab
    vmem = pl.BlockSpec(memory_space=pltpu.VMEM)
    smem = pl.BlockSpec(memory_space=pltpu.SMEM)
    index = jnp.stack([core, here]).astype(jnp.int32)
    return pl.pallas_call(
        functools.partial(up_kernel, width_cols=width_cols),
        out_shape=jax.ShapeDtypeStruct((2 * rows, 2 * width_cols, outs), jnp.bfloat16),
        in_specs=[smem, vmem, vmem, vmem],
        out_specs=vmem,
        scratch_shapes=[pltpu.VMEM((outs, packed_width), jnp.bfloat16), pltpu.VMEM((channels, positions), act.dtype)],
        cost_estimate=pl.CostEstimate(
            flops=2 * positions * channels * 4 * outs, transcendentals=0,
            bytes_accessed=act.size * 2 + 2 * own.size * 2 + rows * width_cols * 4 * outs * 2),
    )(index, act, own, other)


def ring_gather(block, axis):
    chips = lax.axis_size(axis)
    step_up = [(i, (i - 1) % chips) for i in range(chips)]
    step_down = [(i, (i + 1) % chips) for i in range(chips)]
    ahead, behind = block, block
    from_ahead, from_behind = [], []
    for k in range(1, chips // 2 + 1):
        ahead = lax.ppermute(ahead, axis, step_up)
        from_ahead.append(ahead)
        if k < chips - chips // 2:
            behind = lax.ppermute(behind, axis, step_down)
            from_behind.append(behind)
    return jnp.stack([block] + from_ahead + from_behind[::-1])


def body(coarse, conv_weight, conv_bias, norm_gain, norm_shift, up_weight, up_bias):
    chips = lax.axis_size("z")
    core = lax.axis_index("core")
    _, width_cols, channels = coarse.shape
    outputs = conv_weight.shape[0]
    slice_out = up_weight.shape[0]

    whole = lax.all_gather(coarse, ("z", "core"), axis=0, tiled=True)
    height = whole.shape[0]
    flat = up_weight.reshape(slice_out, -1)
    packed = jnp.concatenate([flat, jnp.pad(up_bias[:, None], ((0, 0), (0, 127)))], axis=1)
    packed_z = ring_gather(packed, "z")
    packed_other = lax.ppermute(packed_z, "core", [(0, 1), (1, 0)])

    activated = conv_norm(whole, conv_weight, conv_bias, norm_gain, norm_shift, chips)
    chip_rows = lax.all_to_all(activated, "z", split_axis=0, concat_axis=0, tiled=True)
    chip_rows = chip_rows.reshape(-1, chip_rows.shape[2])
    both = lax.all_gather(chip_rows, "core", axis=0, tiled=True)
    half = coarse.shape[0]
    fine = up_conv(core, lax.axis_index("z"), both, packed_z, packed_other, half)
    return fine.reshape(2 * half, 2 * width_cols, -1)


def solution(mesh):
    grp, sp = mesh.devices.shape
    fine_mesh = Mesh(mesh.devices.reshape(grp, sp // 2, 2), ("grp", "z", "core"))
    rows = ("grp", "z", "core")
    chans = ("z", "core")
    return jax.shard_map(
        body,
        mesh=fine_mesh,
        in_specs=(
            P(rows, None, None),
            P(chans, None, None, None),
            P(chans),
            P(chans),
            P(chans),
            P(chans, None, None, None),
            P(chans),
        ),
        out_specs=P(rows, None, None),
        check_vma=False,
    )
```

```python
import functools

import jax
import jax.numpy as jnp
from jax import lax
from jax.experimental import pallas as pl
from jax.experimental.pallas import tpu as pltpu
from jax.sharding import Mesh, PartitionSpec as P

GSIZE = 32


def conv_norm_kernel(x_ref, w_ref, bias_ref, gain_ref, shift_ref, out_ref, *, height, width_cols):
    outputs = out_ref.shape[1]
    positions = height * width_cols
    taps = lax.dot_general(w_ref[...], x_ref[...], (((1,), (1,)), ((), ())),
                           preferred_element_type=jnp.float32)
    pos = lax.broadcasted_iota(jnp.int32, (1, positions), 1)
    row = pos // width_cols
    col = pos % width_cols
    acc = jnp.zeros((outputs, positions), jnp.float32)
    for t in range(9):
        r, s = divmod(t, 3)
        off = (r - 1) * width_cols + (s - 1)
        part = taps[t * outputs:(t + 1) * outputs, :]
        if off:
            part = pltpu.roll(part, (-off) % positions, 1)
        valid = ((row + (r - 1) >= 0) & (row + (r - 1) < height)
                 & (col + (s - 1) >= 0) & (col + (s - 1) < width_cols))
        acc = acc + jnp.where(valid, part, 0.0)
    conv = acc + bias_ref[...]
    groups = outputs // GSIZE
    grouped = conv.reshape(groups, GSIZE, positions)
    count = GSIZE * positions
    centre = jnp.sum(jnp.sum(grouped, axis=2, keepdims=True), axis=1, keepdims=True) / count
    dev = grouped - centre
    spread = jnp.sum(jnp.sum(dev * dev, axis=2, keepdims=True), axis=1, keepdims=True) / count
    normed = (dev * lax.rsqrt(spread + 1e-05)).reshape(outputs, positions)
    v = normed * gain_ref[...] + shift_ref[...]
    act = (v / (1.0 + jnp.exp(-v))).astype(out_ref.dtype)
    chips, _, span = out_ref.shape
    for chip in range(chips):
        out_ref[chip] = act[:, chip * span:(chip + 1) * span]


def conv_norm(whole, conv_weight, conv_bias, norm_gain, norm_shift, chips):
    height, width_cols, channels = whole.shape
    outputs = conv_weight.shape[0]
    x = whole.reshape(height * width_cols, channels)
    w = jnp.transpose(conv_weight.reshape(outputs, 9, channels), (1, 0, 2)).reshape(9 * outputs, channels)
    col = lambda v: v.astype(jnp.float32).reshape(outputs, 1)
    vmem = pl.BlockSpec(memory_space=pltpu.VMEM)
    return pl.pallas_call(
        functools.partial(conv_norm_kernel, height=height, width_cols=width_cols),
        out_shape=jax.ShapeDtypeStruct((chips, outputs, height * width_cols // chips), jnp.bfloat16),
        in_specs=[vmem] * 5,
        out_specs=vmem,
        cost_estimate=pl.CostEstimate(
            flops=2 * height * width_cols * channels * 9 * outputs,
            transcendentals=height * width_cols * outputs,
            bytes_accessed=x.size * 2 + w.size * 2 + outputs * height * width_cols * 2),
    )(x, w, col(conv_bias), col(norm_gain), col(norm_shift))


def assemble_kernel(index_ref, own_ref, other_ref, wnat_ref):
    chips, slab, _ = own_ref.shape
    core = index_ref[0]
    here = index_ref[1]
    for m in range(chips):
        chip = (here + m) % chips
        mine = pl.multiple_of(2 * slab * chip + slab * core, slab)
        theirs = pl.multiple_of(2 * slab * chip + slab * (1 - core), slab)
        wnat_ref[pl.ds(mine, slab), :] = own_ref[m]
        wnat_ref[pl.ds(theirs, slab), :] = other_ref[m]


def assemble(index, own, other):
    chips, slab, packed_width = own.shape
    vmem = pl.BlockSpec(memory_space=pltpu.VMEM)
    smem = pl.BlockSpec(memory_space=pltpu.SMEM)
    return pl.pallas_call(
        assemble_kernel,
        out_shape=jax.ShapeDtypeStruct((2 * chips * slab, packed_width), own.dtype),
        in_specs=[smem, vmem, vmem],
        out_specs=vmem,
        cost_estimate=pl.CostEstimate(flops=0, transcendentals=0, bytes_accessed=4 * own.size * 2),
    )(index, own, other)


def up_kernel(index_ref, act_ref, wnat_ref, out_ref, actn_ref, *, width_cols):
    outs, packed_width = wnat_ref.shape
    channels, positions = act_ref.shape
    chips = outs // 32
    block = channels // (2 * chips)
    core = index_ref[0]
    for c in range(2):
        for z in range(chips):
            actn_ref[pl.ds((2 * z + c) * block, block), :] = act_ref[pl.ds((c * chips + z) * block, block), :]
    rows = out_ref.shape[0] // 2
    nn = (((1,), (0,)), ((), ()))
    sub = lax.broadcasted_iota(jnp.int32, (packed_width - 4 * channels, positions), 0)
    ones = jnp.where(sub == 0, 1.0, 0.0).astype(actn_ref.dtype)
    bias = lax.dot_general(wnat_ref[:, pl.ds(4 * channels, packed_width - 4 * channels)], ones, nn,
                           preferred_element_type=jnp.float32)
    act = actn_ref[...]
    span = rows * width_cols
    dest = lax.broadcasted_iota(jnp.int32, (2 * width_cols, 2 * width_cols), 0)
    src = lax.broadcasted_iota(jnp.int32, (2 * width_cols, 2 * width_cols), 1)
    interleave = jnp.where(src == (dest % 2) * width_cols + dest // 2, 1.0, 0.0).astype(out_ref.dtype)
    for a in range(2):
        phases = []
        for b in range(2):
            res = lax.dot_general(wnat_ref[:, pl.ds((2 * a + b) * channels, channels)], act, nn,
                                  preferred_element_type=jnp.float32)
            res = jnp.transpose(res + bias).astype(out_ref.dtype)
            phases.append(jnp.where(core == 0, res[:span], res[span:]))
        for i in range(rows):
            stacked = jnp.concatenate([p[i * width_cols:(i + 1) * width_cols] for p in phases], axis=0)
            out_ref[2 * i + a] = jnp.dot(interleave, stacked, preferred_element_type=jnp.float32).astype(out_ref.dtype)


def up_conv(index, act, wnat, rows):
    channels, positions = act.shape
    width_cols = positions // (2 * rows)
    outs, packed_width = wnat.shape
    vmem = pl.BlockSpec(memory_space=pltpu.VMEM)
    smem = pl.BlockSpec(memory_space=pltpu.SMEM)
    return pl.pallas_call(
        functools.partial(up_kernel, width_cols=width_cols),
        out_shape=jax.ShapeDtypeStruct((2 * rows, 2 * width_cols, outs), jnp.bfloat16),
        in_specs=[smem, vmem, vmem],
        out_specs=vmem,
        scratch_shapes=[pltpu.VMEM((channels, positions), act.dtype)],
        cost_estimate=pl.CostEstimate(
            flops=2 * positions * channels * 4 * outs, transcendentals=0,
            bytes_accessed=act.size * 2 + wnat.size * 2 + rows * width_cols * 4 * outs * 2),
    )(index, act, wnat)


def ring_gather(block, axis):
    chips = lax.axis_size(axis)
    step_up = [(i, (i - 1) % chips) for i in range(chips)]
    step_down = [(i, (i + 1) % chips) for i in range(chips)]
    ahead, behind = block, block
    from_ahead, from_behind = [], []
    for k in range(1, chips // 2 + 1):
        ahead = lax.ppermute(ahead, axis, step_up)
        from_ahead.append(ahead)
        if k < chips - chips // 2:
            behind = lax.ppermute(behind, axis, step_down)
            from_behind.append(behind)
    return jnp.stack([block] + from_ahead + from_behind[::-1])


def body(coarse, conv_weight, conv_bias, norm_gain, norm_shift, up_weight, up_bias):
    chips = lax.axis_size("z")
    core = lax.axis_index("core")
    _, width_cols, channels = coarse.shape
    outputs = conv_weight.shape[0]
    slice_out = up_weight.shape[0]

    whole = lax.all_gather(coarse, ("z", "core"), axis=0, tiled=True)
    height = whole.shape[0]
    flat = up_weight.reshape(slice_out, -1)
    packed = jnp.concatenate([flat, jnp.pad(up_bias[:, None], ((0, 0), (0, 127)))], axis=1)
    packed_z = ring_gather(packed, "z")
    packed_other = lax.ppermute(packed_z, "core", [(0, 1), (1, 0)])
    index = jnp.stack([core, lax.axis_index("z")]).astype(jnp.int32)
    wnat = assemble(index, packed_z, packed_other)

    activated = conv_norm(whole, conv_weight, conv_bias, norm_gain, norm_shift, chips)
    chip_rows = lax.all_to_all(activated, "z", split_axis=0, concat_axis=0, tiled=True)
    chip_rows = chip_rows.reshape(-1, chip_rows.shape[2])
    both = lax.all_gather(chip_rows, "core", axis=0, tiled=True)
    half = coarse.shape[0]
    fine = up_conv(index, both, wnat, half)
    return fine.reshape(2 * half, 2 * width_cols, -1)


def solution(mesh):
    grp, sp = mesh.devices.shape
    fine_mesh = Mesh(mesh.devices.reshape(grp, sp // 2, 2), ("grp", "z", "core"))
    rows = ("grp", "z", "core")
    chans = ("z", "core")
    return jax.shard_map(
        body,
        mesh=fine_mesh,
        in_specs=(
            P(rows, None, None),
            P(chans, None, None, None),
            P(chans),
            P(chans),
            P(chans),
            P(chans, None, None, None),
            P(chans),
        ),
        out_specs=P(rows, None, None),
        check_vma=False,
    )
```

```python
import functools

import jax
import jax.numpy as jnp
from jax import lax
from jax.experimental import pallas as pl
from jax.experimental.pallas import tpu as pltpu
from jax.sharding import Mesh, PartitionSpec as P

GSIZE = 32


def conv_norm_kernel(x_ref, w_ref, bias_ref, gain_ref, shift_ref, out_ref, *, height, width_cols):
    outputs = out_ref.shape[1]
    positions = height * width_cols
    taps = lax.dot_general(w_ref[...], x_ref[...], (((1,), (1,)), ((), ())),
                           preferred_element_type=jnp.float32)
    pos = lax.broadcasted_iota(jnp.int32, (1, positions), 1)
    row = pos // width_cols
    col = pos % width_cols
    acc = jnp.zeros((outputs, positions), jnp.float32)
    for t in range(9):
        r, s = divmod(t, 3)
        off = (r - 1) * width_cols + (s - 1)
        part = taps[t * outputs:(t + 1) * outputs, :]
        if off:
            part = pltpu.roll(part, (-off) % positions, 1)
        valid = ((row + (r - 1) >= 0) & (row + (r - 1) < height)
                 & (col + (s - 1) >= 0) & (col + (s - 1) < width_cols))
        acc = acc + jnp.where(valid, part, 0.0)
    conv = acc + bias_ref[...]
    groups = outputs // GSIZE
    grouped = conv.reshape(groups, GSIZE, positions)
    count = GSIZE * positions
    centre = jnp.sum(jnp.sum(grouped, axis=2, keepdims=True), axis=1, keepdims=True) / count
    dev = grouped - centre
    spread = jnp.sum(jnp.sum(dev * dev, axis=2, keepdims=True), axis=1, keepdims=True) / count
    normed = (dev * lax.rsqrt(spread + 1e-05)).reshape(outputs, positions)
    v = normed * gain_ref[...] + shift_ref[...]
    act = (v / (1.0 + jnp.exp(-v))).astype(out_ref.dtype)
    chips, _, span = out_ref.shape
    for chip in range(chips):
        out_ref[chip] = act[:, chip * span:(chip + 1) * span]


def conv_norm(whole, conv_weight, conv_bias, norm_gain, norm_shift, chips):
    height, width_cols, channels = whole.shape
    outputs = conv_weight.shape[0]
    x = whole.reshape(height * width_cols, channels)
    w = jnp.transpose(conv_weight.reshape(outputs, 9, channels), (1, 0, 2)).reshape(9 * outputs, channels)
    col = lambda v: v.astype(jnp.float32).reshape(outputs, 1)
    vmem = pl.BlockSpec(memory_space=pltpu.VMEM)
    return pl.pallas_call(
        functools.partial(conv_norm_kernel, height=height, width_cols=width_cols),
        out_shape=jax.ShapeDtypeStruct((chips, outputs, height * width_cols // chips), jnp.bfloat16),
        in_specs=[vmem] * 5,
        out_specs=vmem,
        cost_estimate=pl.CostEstimate(
            flops=2 * height * width_cols * channels * 9 * outputs,
            transcendentals=height * width_cols * outputs,
            bytes_accessed=x.size * 2 + w.size * 2 + outputs * height * width_cols * 2),
    )(x, w, col(conv_bias), col(norm_gain), col(norm_shift))


def assemble_kernel(index_ref, own_ref, other_ref, wnat_ref):
    chips, slab, _ = own_ref.shape
    core = index_ref[0]
    here = index_ref[1]
    for m in range(chips):
        chip = (here + m) % chips
        mine = pl.multiple_of(2 * slab * chip + slab * core, slab)
        theirs = pl.multiple_of(2 * slab * chip + slab * (1 - core), slab)
        wnat_ref[pl.ds(mine, slab), :] = own_ref[m]
        wnat_ref[pl.ds(theirs, slab), :] = other_ref[m]


def assemble(index, own, other):
    chips, slab, packed_width = own.shape
    vmem = pl.BlockSpec(memory_space=pltpu.VMEM)
    smem = pl.BlockSpec(memory_space=pltpu.SMEM)
    return pl.pallas_call(
        assemble_kernel,
        out_shape=jax.ShapeDtypeStruct((2 * chips * slab, packed_width), own.dtype),
        in_specs=[smem, vmem, vmem],
        out_specs=vmem,
        cost_estimate=pl.CostEstimate(flops=0, transcendentals=0, bytes_accessed=4 * own.size * 2),
    )(index, own, other)


def up_kernel(index_ref, act_ref, wnat_ref, out_ref, actn_ref, *, width_cols):
    outs, packed_width = wnat_ref.shape
    channels, positions = act_ref.shape
    chips = outs // 32
    block = channels // (2 * chips)
    core = index_ref[0]
    rows = out_ref.shape[0] // 2
    span = rows * width_cols
    lanes = actn_ref.shape[1]
    skip = positions - lanes
    for c in range(2):
        for z in range(chips):
            rows_in = act_ref[pl.ds((c * chips + z) * block, block), :]
            actn_ref[pl.ds((2 * z + c) * block, block), :] = jnp.where(core == 0, rows_in[:, :lanes], rows_in[:, skip:])
    nn = (((1,), (0,)), ((), ()))
    sub = lax.broadcasted_iota(jnp.int32, (packed_width - 4 * channels, lanes), 0)
    ones = jnp.where(sub == 0, 1.0, 0.0).astype(actn_ref.dtype)
    bias = lax.dot_general(wnat_ref[:, pl.ds(4 * channels, packed_width - 4 * channels)], ones, nn,
                           preferred_element_type=jnp.float32)
    act = actn_ref[...]
    first = lanes - span
    dest = lax.broadcasted_iota(jnp.int32, (2 * width_cols, 2 * width_cols), 0)
    src = lax.broadcasted_iota(jnp.int32, (2 * width_cols, 2 * width_cols), 1)
    interleave = jnp.where(src == (dest % 2) * width_cols + dest // 2, 1.0, 0.0).astype(out_ref.dtype)
    for a in range(2):
        phases = []
        for b in range(2):
            res = lax.dot_general(wnat_ref[:, pl.ds((2 * a + b) * channels, channels)], act, nn,
                                  preferred_element_type=jnp.float32)
            res = jnp.transpose(res + bias).astype(out_ref.dtype)
            phases.append(jnp.where(core == 0, res[:span], res[first:]))
        for i in range(rows):
            stacked = jnp.concatenate([p[i * width_cols:(i + 1) * width_cols] for p in phases], axis=0)
            out_ref[2 * i + a] = jnp.dot(interleave, stacked, preferred_element_type=jnp.float32).astype(out_ref.dtype)


def up_conv(index, act, wnat, rows):
    channels, positions = act.shape
    width_cols = positions // (2 * rows)
    outs, packed_width = wnat.shape
    vmem = pl.BlockSpec(memory_space=pltpu.VMEM)
    smem = pl.BlockSpec(memory_space=pltpu.SMEM)
    return pl.pallas_call(
        functools.partial(up_kernel, width_cols=width_cols),
        out_shape=jax.ShapeDtypeStruct((2 * rows, 2 * width_cols, outs), jnp.bfloat16),
        in_specs=[smem, vmem, vmem],
        out_specs=vmem,
        scratch_shapes=[pltpu.VMEM((channels, -(-positions // 2 // 128) * 128), act.dtype)],
        cost_estimate=pl.CostEstimate(
            flops=2 * positions * channels * 4 * outs, transcendentals=0,
            bytes_accessed=act.size * 2 + wnat.size * 2 + rows * width_cols * 4 * outs * 2),
    )(index, act, wnat)


def ring_gather(block, axis):
    chips = lax.axis_size(axis)
    step_up = [(i, (i - 1) % chips) for i in range(chips)]
    step_down = [(i, (i + 1) % chips) for i in range(chips)]
    ahead, behind = block, block
    from_ahead, from_behind = [], []
    for k in range(1, chips // 2 + 1):
        ahead = lax.ppermute(ahead, axis, step_up)
        from_ahead.append(ahead)
        if k < chips - chips // 2:
            behind = lax.ppermute(behind, axis, step_down)
            from_behind.append(behind)
    return jnp.stack([block] + from_ahead + from_behind[::-1])


def body(coarse, conv_weight, conv_bias, norm_gain, norm_shift, up_weight, up_bias):
    chips = lax.axis_size("z")
    core = lax.axis_index("core")
    _, width_cols, channels = coarse.shape
    outputs = conv_weight.shape[0]
    slice_out = up_weight.shape[0]

    whole = lax.all_gather(coarse, ("z", "core"), axis=0, tiled=True)
    height = whole.shape[0]
    flat = up_weight.reshape(slice_out, -1)
    packed = jnp.concatenate([flat, jnp.pad(up_bias[:, None], ((0, 0), (0, 127)))], axis=1)
    packed_z = ring_gather(packed, "z")
    packed_other = lax.ppermute(packed_z, "core", [(0, 1), (1, 0)])
    index = jnp.stack([core, lax.axis_index("z")]).astype(jnp.int32)
    wnat = assemble(index, packed_z, packed_other)

    activated = conv_norm(whole, conv_weight, conv_bias, norm_gain, norm_shift, chips)
    chip_rows = lax.all_to_all(activated, "z", split_axis=0, concat_axis=0, tiled=True)
    chip_rows = chip_rows.reshape(-1, chip_rows.shape[2])
    both = lax.all_gather(chip_rows, "core", axis=0, tiled=True)
    half = coarse.shape[0]
    fine = up_conv(index, both, wnat, half)
    return fine.reshape(2 * half, 2 * width_cols, -1)


def solution(mesh):
    grp, sp = mesh.devices.shape
    fine_mesh = Mesh(mesh.devices.reshape(grp, sp // 2, 2), ("grp", "z", "core"))
    rows = ("grp", "z", "core")
    chans = ("z", "core")
    return jax.shard_map(
        body,
        mesh=fine_mesh,
        in_specs=(
            P(rows, None, None),
            P(chans, None, None, None),
            P(chans),
            P(chans),
            P(chans),
            P(chans, None, None, None),
            P(chans),
        ),
        out_specs=P(rows, None, None),
        check_vma=False,
    )
```

```python
import functools

import jax
import jax.numpy as jnp
from jax import lax
from jax.experimental import pallas as pl
from jax.experimental.pallas import tpu as pltpu
from jax.sharding import Mesh, PartitionSpec as P

GSIZE = 32


def conv_norm_kernel(x_hbm, w_ref, bias_ref, gain_ref, shift_ref, out_ref, x_buf, taps_ref, sems, *,
                     height, width_cols):
    outputs = out_ref.shape[1]
    positions = height * width_cols
    pieces, chunk, _ = x_buf.shape
    copies = [pltpu.make_async_copy(x_hbm.at[pl.ds(p * chunk, chunk)], x_buf.at[p], sems.at[p])
              for p in range(pieces)]
    for copy in copies:
        copy.start()
    for p in range(pieces):
        copies[p].wait()
        taps_ref[:, pl.ds(p * chunk, chunk)] = lax.dot_general(
            w_ref[...], x_buf[p], (((1,), (1,)), ((), ())), preferred_element_type=jnp.float32)
    taps = taps_ref[...]
    pos = lax.broadcasted_iota(jnp.int32, (1, positions), 1)
    row = pos // width_cols
    col = pos % width_cols
    acc = jnp.zeros((outputs, positions), jnp.float32)
    for t in range(9):
        r, s = divmod(t, 3)
        off = (r - 1) * width_cols + (s - 1)
        part = taps[t * outputs:(t + 1) * outputs, :]
        if off:
            part = pltpu.roll(part, (-off) % positions, 1)
        valid = ((row + (r - 1) >= 0) & (row + (r - 1) < height)
                 & (col + (s - 1) >= 0) & (col + (s - 1) < width_cols))
        acc = acc + jnp.where(valid, part, 0.0)
    conv = acc + bias_ref[...]
    groups = outputs // GSIZE
    grouped = conv.reshape(groups, GSIZE, positions)
    count = GSIZE * positions
    centre = jnp.sum(jnp.sum(grouped, axis=2, keepdims=True), axis=1, keepdims=True) / count
    dev = grouped - centre
    spread = jnp.sum(jnp.sum(dev * dev, axis=2, keepdims=True), axis=1, keepdims=True) / count
    normed = (dev * lax.rsqrt(spread + 1e-05)).reshape(outputs, positions)
    v = normed * gain_ref[...] + shift_ref[...]
    act = (v / (1.0 + jnp.exp(-v))).astype(out_ref.dtype)
    chips, _, span = out_ref.shape
    for chip in range(chips):
        out_ref[chip] = act[:, chip * span:(chip + 1) * span]


def conv_norm(whole, conv_weight, conv_bias, norm_gain, norm_shift, chips):
    height, width_cols, channels = whole.shape
    outputs = conv_weight.shape[0]
    x = whole.reshape(height * width_cols, channels)
    w = jnp.transpose(conv_weight.reshape(outputs, 9, channels), (1, 0, 2)).reshape(9 * outputs, channels)
    col = lambda v: v.astype(jnp.float32).reshape(outputs, 1)
    vmem = pl.BlockSpec(memory_space=pltpu.VMEM)
    return pl.pallas_call(
        functools.partial(conv_norm_kernel, height=height, width_cols=width_cols),
        out_shape=jax.ShapeDtypeStruct((chips, outputs, height * width_cols // chips), jnp.bfloat16),
        in_specs=[pl.BlockSpec(memory_space=pl.ANY)] + [vmem] * 4,
        out_specs=vmem,
        scratch_shapes=[pltpu.VMEM((4, height * width_cols // 4, channels), whole.dtype),
                        pltpu.VMEM((9 * outputs, height * width_cols), jnp.float32),
                        pltpu.SemaphoreType.DMA((4,))],
        cost_estimate=pl.CostEstimate(
            flops=2 * height * width_cols * channels * 9 * outputs,
            transcendentals=height * width_cols * outputs,
            bytes_accessed=x.size * 2 + w.size * 2 + outputs * height * width_cols * 2),
    )(x, w, col(conv_bias), col(norm_gain), col(norm_shift))


def assemble_kernel(index_ref, own_ref, other_ref, wnat_ref):
    chips, slab, _ = own_ref.shape
    core = index_ref[0]
    here = index_ref[1]
    for m in range(chips):
        chip = (here + m) % chips
        mine = pl.multiple_of(2 * slab * chip + slab * core, slab)
        theirs = pl.multiple_of(2 * slab * chip + slab * (1 - core), slab)
        wnat_ref[pl.ds(mine, slab), :] = own_ref[m]
        wnat_ref[pl.ds(theirs, slab), :] = other_ref[m]


def assemble(index, own, other):
    chips, slab, packed_width = own.shape
    vmem = pl.BlockSpec(memory_space=pltpu.VMEM)
    smem = pl.BlockSpec(memory_space=pltpu.SMEM)
    return pl.pallas_call(
        assemble_kernel,
        out_shape=jax.ShapeDtypeStruct((2 * chips * slab, packed_width), own.dtype),
        in_specs=[smem, vmem, vmem],
        out_specs=vmem,
        cost_estimate=pl.CostEstimate(flops=0, transcendentals=0, bytes_accessed=4 * own.size * 2),
    )(index, own, other)


def up_kernel(index_ref, act_ref, wnat_ref, out_ref, actn_ref, *, width_cols):
    outs, packed_width = wnat_ref.shape
    channels, positions = act_ref.shape
    chips = outs // 32
    block = channels // (2 * chips)
    core = index_ref[0]
    rows = out_ref.shape[0] // 2
    span = rows * width_cols
    lanes = actn_ref.shape[1]
    skip = positions - lanes
    for c in range(2):
        for z in range(chips):
            rows_in = act_ref[pl.ds((c * chips + z) * block, block), :]
            actn_ref[pl.ds((2 * z + c) * block, block), :] = jnp.where(core == 0, rows_in[:, :lanes], rows_in[:, skip:])
    nn = (((1,), (0,)), ((), ()))
    sub = lax.broadcasted_iota(jnp.int32, (packed_width - 4 * channels, lanes), 0)
    ones = jnp.where(sub == 0, 1.0, 0.0).astype(actn_ref.dtype)
    bias = lax.dot_general(wnat_ref[:, pl.ds(4 * channels, packed_width - 4 * channels)], ones, nn,
                           preferred_element_type=jnp.float32)
    act = actn_ref[...]
    first = lanes - span
    dest = lax.broadcasted_iota(jnp.int32, (2 * width_cols, 2 * width_cols), 0)
    src = lax.broadcasted_iota(jnp.int32, (2 * width_cols, 2 * width_cols), 1)
    interleave = jnp.where(src == (dest % 2) * width_cols + dest // 2, 1.0, 0.0).astype(out_ref.dtype)
    for a in range(2):
        phases = []
        for b in range(2):
            res = lax.dot_general(wnat_ref[:, pl.ds((2 * a + b) * channels, channels)], act, nn,
                                  preferred_element_type=jnp.float32)
            res = jnp.transpose(res + bias).astype(out_ref.dtype)
            phases.append(jnp.where(core == 0, res[:span], res[first:]))
        for i in range(rows):
            stacked = jnp.concatenate([p[i * width_cols:(i + 1) * width_cols] for p in phases], axis=0)
            out_ref[2 * i + a] = jnp.dot(interleave, stacked, preferred_element_type=jnp.float32).astype(out_ref.dtype)


def up_conv(index, act, wnat, rows):
    channels, positions = act.shape
    width_cols = positions // (2 * rows)
    outs, packed_width = wnat.shape
    vmem = pl.BlockSpec(memory_space=pltpu.VMEM)
    smem = pl.BlockSpec(memory_space=pltpu.SMEM)
    return pl.pallas_call(
        functools.partial(up_kernel, width_cols=width_cols),
        out_shape=jax.ShapeDtypeStruct((2 * rows, 2 * width_cols, outs), jnp.bfloat16),
        in_specs=[smem, vmem, vmem],
        out_specs=vmem,
        scratch_shapes=[pltpu.VMEM((channels, -(-positions // 2 // 128) * 128), act.dtype)],
        cost_estimate=pl.CostEstimate(
            flops=2 * positions * channels * 4 * outs, transcendentals=0,
            bytes_accessed=act.size * 2 + wnat.size * 2 + rows * width_cols * 4 * outs * 2),
    )(index, act, wnat)


def ring_gather(block, axis):
    chips = lax.axis_size(axis)
    step_up = [(i, (i - 1) % chips) for i in range(chips)]
    step_down = [(i, (i + 1) % chips) for i in range(chips)]
    ahead, behind = block, block
    from_ahead, from_behind = [], []
    for k in range(1, chips // 2 + 1):
        ahead = lax.ppermute(ahead, axis, step_up)
        from_ahead.append(ahead)
        if k < chips - chips // 2:
            behind = lax.ppermute(behind, axis, step_down)
            from_behind.append(behind)
    return jnp.stack([block] + from_ahead + from_behind[::-1])


def body(coarse, conv_weight, conv_bias, norm_gain, norm_shift, up_weight, up_bias):
    chips = lax.axis_size("z")
    core = lax.axis_index("core")
    _, width_cols, channels = coarse.shape
    outputs = conv_weight.shape[0]
    slice_out = up_weight.shape[0]

    whole = lax.all_gather(coarse, ("z", "core"), axis=0, tiled=True)
    height = whole.shape[0]
    flat = up_weight.reshape(slice_out, -1)
    packed = jnp.concatenate([flat, jnp.pad(up_bias[:, None], ((0, 0), (0, 127)))], axis=1)
    packed_z = ring_gather(packed, "z")
    packed_other = lax.ppermute(packed_z, "core", [(0, 1), (1, 0)])
    index = jnp.stack([core, lax.axis_index("z")]).astype(jnp.int32)
    wnat = assemble(index, packed_z, packed_other)

    activated = conv_norm(whole, conv_weight, conv_bias, norm_gain, norm_shift, chips)
    chip_rows = lax.all_to_all(activated, "z", split_axis=0, concat_axis=0, tiled=True)
    chip_rows = chip_rows.reshape(-1, chip_rows.shape[2])
    both = lax.all_gather(chip_rows, "core", axis=0, tiled=True)
    half = coarse.shape[0]
    fine = up_conv(index, both, wnat, half)
    return fine.reshape(2 * half, 2 * width_cols, -1)


def solution(mesh):
    grp, sp = mesh.devices.shape
    fine_mesh = Mesh(mesh.devices.reshape(grp, sp // 2, 2), ("grp", "z", "core"))
    rows = ("grp", "z", "core")
    chans = ("z", "core")
    return jax.shard_map(
        body,
        mesh=fine_mesh,
        in_specs=(
            P(rows, None, None),
            P(chans, None, None, None),
            P(chans),
            P(chans),
            P(chans),
            P(chans, None, None, None),
            P(chans),
        ),
        out_specs=P(rows, None, None),
        check_vma=False,
    )
```

```python
import functools

import jax
import jax.numpy as jnp
from jax import lax
from jax.experimental import pallas as pl
from jax.experimental.pallas import tpu as pltpu
from jax.sharding import Mesh, PartitionSpec as P

GSIZE = 32


def conv_norm_kernel(x_ref, w_ref, bias_ref, gain_ref, shift_ref, out_ref, *, height, width_cols):
    outputs = out_ref.shape[1]
    positions = height * width_cols
    taps = jnp.transpose(lax.dot_general(x_ref[...], w_ref[...], (((1,), (0,)), ((), ())),
                                         preferred_element_type=jnp.float32))
    pos = lax.broadcasted_iota(jnp.int32, (1, positions), 1)
    row = pos // width_cols
    col = pos % width_cols
    acc = jnp.zeros((outputs, positions), jnp.float32)
    for t in range(9):
        r, s = divmod(t, 3)
        off = (r - 1) * width_cols + (s - 1)
        part = taps[t * outputs:(t + 1) * outputs, :]
        if off:
            part = pltpu.roll(part, (-off) % positions, 1)
        valid = ((row + (r - 1) >= 0) & (row + (r - 1) < height)
                 & (col + (s - 1) >= 0) & (col + (s - 1) < width_cols))
        acc = acc + jnp.where(valid, part, 0.0)
    conv = acc + bias_ref[...]
    groups = outputs // GSIZE
    grouped = conv.reshape(groups, GSIZE, positions)
    count = GSIZE * positions
    centre = jnp.sum(jnp.sum(grouped, axis=2, keepdims=True), axis=1, keepdims=True) / count
    dev = grouped - centre
    spread = jnp.sum(jnp.sum(dev * dev, axis=2, keepdims=True), axis=1, keepdims=True) / count
    normed = (dev * lax.rsqrt(spread + 1e-05)).reshape(outputs, positions)
    v = normed * gain_ref[...] + shift_ref[...]
    act = (v / (1.0 + jnp.exp(-v))).astype(out_ref.dtype)
    chips, _, span = out_ref.shape
    for chip in range(chips):
        out_ref[chip] = act[:, chip * span:(chip + 1) * span]


def conv_norm(whole, conv_weight, conv_bias, norm_gain, norm_shift, chips):
    height, width_cols, channels = whole.shape
    outputs = conv_weight.shape[0]
    x = whole.reshape(height * width_cols, channels)
    w = jnp.transpose(conv_weight.reshape(outputs, 9, channels), (1, 0, 2)).reshape(9 * outputs, channels)
    w = jnp.transpose(jnp.pad(w, ((0, -(-9 * outputs // 128) * 128 - 9 * outputs), (0, 0))))
    col = lambda v: v.astype(jnp.float32).reshape(outputs, 1)
    vmem = pl.BlockSpec(memory_space=pltpu.VMEM)
    return pl.pallas_call(
        functools.partial(conv_norm_kernel, height=height, width_cols=width_cols),
        out_shape=jax.ShapeDtypeStruct((chips, outputs, height * width_cols // chips), jnp.bfloat16),
        in_specs=[vmem] * 5,
        out_specs=vmem,
        cost_estimate=pl.CostEstimate(
            flops=2 * height * width_cols * channels * 9 * outputs,
            transcendentals=height * width_cols * outputs,
            bytes_accessed=x.size * 2 + w.size * 2 + outputs * height * width_cols * 2),
    )(x, w, col(conv_bias), col(norm_gain), col(norm_shift))


def assemble_kernel(index_ref, own_ref, other_ref, wnat_ref):
    chips, slab, _ = own_ref.shape
    core = index_ref[0]
    here = index_ref[1]
    for m in range(chips):
        chip = (here + m) % chips
        mine = pl.multiple_of(2 * slab * chip + slab * core, slab)
        theirs = pl.multiple_of(2 * slab * chip + slab * (1 - core), slab)
        wnat_ref[pl.ds(mine, slab), :] = own_ref[m]
        wnat_ref[pl.ds(theirs, slab), :] = other_ref[m]


def assemble(index, own, other):
    chips, slab, packed_width = own.shape
    vmem = pl.BlockSpec(memory_space=pltpu.VMEM)
    smem = pl.BlockSpec(memory_space=pltpu.SMEM)
    return pl.pallas_call(
        assemble_kernel,
        out_shape=jax.ShapeDtypeStruct((2 * chips * slab, packed_width), own.dtype),
        in_specs=[smem, vmem, vmem],
        out_specs=vmem,
        cost_estimate=pl.CostEstimate(flops=0, transcendentals=0, bytes_accessed=4 * own.size * 2),
    )(index, own, other)


def up_kernel(index_ref, act_ref, wnat_ref, out_ref, actn_ref, *, width_cols):
    outs, packed_width = wnat_ref.shape
    channels, positions = act_ref.shape
    chips = outs // 32
    block = channels // (2 * chips)
    core = index_ref[0]
    rows = out_ref.shape[0] // 2
    span = rows * width_cols
    lanes = actn_ref.shape[1]
    skip = positions - lanes
    for c in range(2):
        for z in range(chips):
            rows_in = act_ref[pl.ds((c * chips + z) * block, block), :]
            actn_ref[pl.ds((2 * z + c) * block, block), :] = jnp.where(core == 0, rows_in[:, :lanes], rows_in[:, skip:])
    nn = (((1,), (0,)), ((), ()))
    sub = lax.broadcasted_iota(jnp.int32, (packed_width - 4 * channels, lanes), 0)
    ones = jnp.where(sub == 0, 1.0, 0.0).astype(actn_ref.dtype)
    bias = lax.dot_general(wnat_ref[:, pl.ds(4 * channels, packed_width - 4 * channels)], ones, nn,
                           preferred_element_type=jnp.float32)
    act = actn_ref[...]
    first = lanes - span
    dest = lax.broadcasted_iota(jnp.int32, (2 * width_cols, 2 * width_cols), 0)
    src = lax.broadcasted_iota(jnp.int32, (2 * width_cols, 2 * width_cols), 1)
    interleave = jnp.where(src == (dest % 2) * width_cols + dest // 2, 1.0, 0.0).astype(out_ref.dtype)
    for a in range(2):
        phases = []
        for b in range(2):
            res = lax.dot_general(wnat_ref[:, pl.ds((2 * a + b) * channels, channels)], act, nn,
                                  preferred_element_type=jnp.float32)
            res = jnp.transpose(res + bias).astype(out_ref.dtype)
            phases.append(jnp.where(core == 0, res[:span], res[first:]))
        for i in range(rows):
            stacked = jnp.concatenate([p[i * width_cols:(i + 1) * width_cols] for p in phases], axis=0)
            out_ref[2 * i + a] = jnp.dot(interleave, stacked, preferred_element_type=jnp.float32).astype(out_ref.dtype)


def up_conv(index, act, wnat, rows):
    channels, positions = act.shape
    width_cols = positions // (2 * rows)
    outs, packed_width = wnat.shape
    vmem = pl.BlockSpec(memory_space=pltpu.VMEM)
    smem = pl.BlockSpec(memory_space=pltpu.SMEM)
    return pl.pallas_call(
        functools.partial(up_kernel, width_cols=width_cols),
        out_shape=jax.ShapeDtypeStruct((2 * rows, 2 * width_cols, outs), jnp.bfloat16),
        in_specs=[smem, vmem, vmem],
        out_specs=vmem,
        scratch_shapes=[pltpu.VMEM((channels, -(-positions // 2 // 128) * 128), act.dtype)],
        cost_estimate=pl.CostEstimate(
            flops=2 * positions * channels * 4 * outs, transcendentals=0,
            bytes_accessed=act.size * 2 + wnat.size * 2 + rows * width_cols * 4 * outs * 2),
    )(index, act, wnat)


def ring_gather(block, axis):
    chips = lax.axis_size(axis)
    step_up = [(i, (i - 1) % chips) for i in range(chips)]
    step_down = [(i, (i + 1) % chips) for i in range(chips)]
    ahead, behind = block, block
    from_ahead, from_behind = [], []
    for k in range(1, chips // 2 + 1):
        ahead = lax.ppermute(ahead, axis, step_up)
        from_ahead.append(ahead)
        if k < chips - chips // 2:
            behind = lax.ppermute(behind, axis, step_down)
            from_behind.append(behind)
    return jnp.stack([block] + from_ahead + from_behind[::-1])


def body(coarse, conv_weight, conv_bias, norm_gain, norm_shift, up_weight, up_bias):
    chips = lax.axis_size("z")
    core = lax.axis_index("core")
    _, width_cols, channels = coarse.shape
    outputs = conv_weight.shape[0]
    slice_out = up_weight.shape[0]

    whole = lax.all_gather(coarse, ("z", "core"), axis=0, tiled=True)
    height = whole.shape[0]
    flat = up_weight.reshape(slice_out, -1)
    packed = jnp.concatenate([flat, jnp.pad(up_bias[:, None], ((0, 0), (0, 127)))], axis=1)
    packed_z = ring_gather(packed, "z")
    packed_other = lax.ppermute(packed_z, "core", [(0, 1), (1, 0)])
    index = jnp.stack([core, lax.axis_index("z")]).astype(jnp.int32)
    wnat = assemble(index, packed_z, packed_other)

    activated = conv_norm(whole, conv_weight, conv_bias, norm_gain, norm_shift, chips)
    chip_rows = lax.all_to_all(activated, "z", split_axis=0, concat_axis=0, tiled=True)
    chip_rows = chip_rows.reshape(-1, chip_rows.shape[2])
    both = lax.all_gather(chip_rows, "core", axis=0, tiled=True)
    half = coarse.shape[0]
    fine = up_conv(index, both, wnat, half)
    return fine.reshape(2 * half, 2 * width_cols, -1)


def solution(mesh):
    grp, sp = mesh.devices.shape
    fine_mesh = Mesh(mesh.devices.reshape(grp, sp // 2, 2), ("grp", "z", "core"))
    rows = ("grp", "z", "core")
    chans = ("z", "core")
    return jax.shard_map(
        body,
        mesh=fine_mesh,
        in_specs=(
            P(rows, None, None),
            P(chans, None, None, None),
            P(chans),
            P(chans),
            P(chans),
            P(chans, None, None, None),
            P(chans),
        ),
        out_specs=P(rows, None, None),
        check_vma=False,
    )
```

```python
import functools

import jax
import jax.numpy as jnp
from jax import lax
from jax.experimental import pallas as pl
from jax.experimental.pallas import tpu as pltpu
from jax.sharding import Mesh, PartitionSpec as P

GSIZE = 32


def conv_norm_kernel(x_ref, w_ref, bias_ref, gain_ref, shift_ref, out_ref, *, height, width_cols):
    outputs = out_ref.shape[1]
    positions = height * width_cols
    taps = lax.dot_general(w_ref[...], x_ref[...], (((1,), (1,)), ((), ())),
                           preferred_element_type=jnp.float32)
    pos = lax.broadcasted_iota(jnp.int32, (1, positions), 1)
    row = pos // width_cols
    col = pos % width_cols
    acc = jnp.zeros((outputs, positions), jnp.float32)
    for t in range(9):
        r, s = divmod(t, 3)
        off = (r - 1) * width_cols + (s - 1)
        part = taps[t * outputs:(t + 1) * outputs, :]
        if off:
            part = pltpu.roll(part, (-off) % positions, 1)
        valid = ((row + (r - 1) >= 0) & (row + (r - 1) < height)
                 & (col + (s - 1) >= 0) & (col + (s - 1) < width_cols))
        acc = acc + jnp.where(valid, part, 0.0)
    conv = acc + bias_ref[...]
    groups = outputs // GSIZE
    grouped = conv.reshape(groups, GSIZE, positions)
    count = GSIZE * positions
    centre = jnp.sum(jnp.sum(grouped, axis=2, keepdims=True), axis=1, keepdims=True) / count
    dev = grouped - centre
    spread = jnp.sum(jnp.sum(dev * dev, axis=2, keepdims=True), axis=1, keepdims=True) / count
    normed = (dev * lax.rsqrt(spread + 1e-05)).reshape(outputs, positions)
    v = normed * gain_ref[...] + shift_ref[...]
    act = (v / (1.0 + jnp.exp(-v))).astype(out_ref.dtype)
    chips, _, span = out_ref.shape
    for chip in range(chips):
        out_ref[chip] = act[:, chip * span:(chip + 1) * span]


def conv_norm(whole, conv_weight, conv_bias, norm_gain, norm_shift, chips):
    height, width_cols, channels = whole.shape
    outputs = conv_weight.shape[0]
    x = whole.reshape(height * width_cols, channels)
    w = jnp.transpose(conv_weight.reshape(outputs, 9, channels), (1, 0, 2)).reshape(9 * outputs, channels)
    col = lambda v: v.astype(jnp.float32).reshape(outputs, 1)
    vmem = pl.BlockSpec(memory_space=pltpu.VMEM)
    return pl.pallas_call(
        functools.partial(conv_norm_kernel, height=height, width_cols=width_cols),
        out_shape=jax.ShapeDtypeStruct((chips, outputs, height * width_cols // chips), jnp.bfloat16),
        in_specs=[vmem] * 5,
        out_specs=vmem,
        cost_estimate=pl.CostEstimate(
            flops=2 * height * width_cols * channels * 9 * outputs,
            transcendentals=height * width_cols * outputs,
            bytes_accessed=x.size * 2 + w.size * 2 + outputs * height * width_cols * 2),
    )(x, w, col(conv_bias), col(norm_gain), col(norm_shift))


def assemble_kernel(index_ref, own_ref, other_ref, wnat_ref):
    chips, slab, _ = own_ref.shape
    core = index_ref[0]
    here = index_ref[1]
    for m in range(chips):
        chip = (here + m) % chips
        mine = pl.multiple_of(2 * slab * chip + slab * core, slab)
        theirs = pl.multiple_of(2 * slab * chip + slab * (1 - core), slab)
        wnat_ref[pl.ds(mine, slab), :] = own_ref[m]
        wnat_ref[pl.ds(theirs, slab), :] = other_ref[m]


def assemble(index, own, other):
    chips, slab, packed_width = own.shape
    vmem = pl.BlockSpec(memory_space=pltpu.VMEM)
    smem = pl.BlockSpec(memory_space=pltpu.SMEM)
    return pl.pallas_call(
        assemble_kernel,
        out_shape=jax.ShapeDtypeStruct((2 * chips * slab, packed_width), own.dtype),
        in_specs=[smem, vmem, vmem],
        out_specs=vmem,
        cost_estimate=pl.CostEstimate(flops=0, transcendentals=0, bytes_accessed=4 * own.size * 2),
    )(index, own, other)


def up_kernel(index_ref, act_ref, wnat_ref, out_ref, actn_ref, *, width_cols):
    outs, packed_width = wnat_ref.shape
    channels, positions = act_ref.shape
    chips = outs // 32
    block = channels // (2 * chips)
    core = index_ref[0]
    rows = out_ref.shape[0] // 2
    span = rows * width_cols
    lanes = actn_ref.shape[1]
    skip = positions - lanes
    for c in range(2):
        for z in range(chips):
            rows_in = act_ref[pl.ds((c * chips + z) * block, block), :]
            actn_ref[pl.ds((2 * z + c) * block, block), :] = jnp.where(core == 0, rows_in[:, :lanes], rows_in[:, skip:])
    nt = (((1,), (1,)), ((), ()))
    lane = lax.broadcasted_iota(jnp.int32, (lanes, packed_width - 4 * channels), 1)
    ones = jnp.where(lane == 0, 1.0, 0.0).astype(actn_ref.dtype)
    bias = lax.dot_general(ones, wnat_ref[:, pl.ds(4 * channels, packed_width - 4 * channels)], nt,
                           preferred_element_type=jnp.float32)
    act = jnp.transpose(actn_ref[...].astype(jnp.float32)).astype(actn_ref.dtype)
    first = lanes - span
    dest = lax.broadcasted_iota(jnp.int32, (2 * width_cols, 2 * width_cols), 0)
    src = lax.broadcasted_iota(jnp.int32, (2 * width_cols, 2 * width_cols), 1)
    interleave = jnp.where(src == (dest % 2) * width_cols + dest // 2, 1.0, 0.0).astype(out_ref.dtype)
    for a in range(2):
        phases = []
        for b in range(2):
            res = lax.dot_general(act, wnat_ref[:, pl.ds((2 * a + b) * channels, channels)], nt,
                                  preferred_element_type=jnp.float32)
            res = (res + bias).astype(out_ref.dtype)
            phases.append(jnp.where(core == 0, res[:span], res[first:]))
        for i in range(rows):
            stacked = jnp.concatenate([p[i * width_cols:(i + 1) * width_cols] for p in phases], axis=0)
            out_ref[2 * i + a] = jnp.dot(interleave, stacked, preferred_element_type=jnp.float32).astype(out_ref.dtype)


def up_conv(index, act, wnat, rows):
    channels, positions = act.shape
    width_cols = positions // (2 * rows)
    outs, packed_width = wnat.shape
    vmem = pl.BlockSpec(memory_space=pltpu.VMEM)
    smem = pl.BlockSpec(memory_space=pltpu.SMEM)
    return pl.pallas_call(
        functools.partial(up_kernel, width_cols=width_cols),
        out_shape=jax.ShapeDtypeStruct((2 * rows, 2 * width_cols, outs), jnp.bfloat16),
        in_specs=[smem, vmem, vmem],
        out_specs=vmem,
        scratch_shapes=[pltpu.VMEM((channels, -(-positions // 2 // 128) * 128), act.dtype)],
        cost_estimate=pl.CostEstimate(
            flops=2 * positions * channels * 4 * outs, transcendentals=0,
            bytes_accessed=act.size * 2 + wnat.size * 2 + rows * width_cols * 4 * outs * 2),
    )(index, act, wnat)


def ring_gather(block, axis):
    chips = lax.axis_size(axis)
    step_up = [(i, (i - 1) % chips) for i in range(chips)]
    step_down = [(i, (i + 1) % chips) for i in range(chips)]
    ahead, behind = block, block
    from_ahead, from_behind = [], []
    for k in range(1, chips // 2 + 1):
        ahead = lax.ppermute(ahead, axis, step_up)
        from_ahead.append(ahead)
        if k < chips - chips // 2:
            behind = lax.ppermute(behind, axis, step_down)
            from_behind.append(behind)
    return jnp.stack([block] + from_ahead + from_behind[::-1])


def body(coarse, conv_weight, conv_bias, norm_gain, norm_shift, up_weight, up_bias):
    chips = lax.axis_size("z")
    core = lax.axis_index("core")
    _, width_cols, channels = coarse.shape
    outputs = conv_weight.shape[0]
    slice_out = up_weight.shape[0]

    whole = lax.all_gather(coarse, ("z", "core"), axis=0, tiled=True)
    height = whole.shape[0]
    flat = up_weight.reshape(slice_out, -1)
    packed = jnp.concatenate([flat, jnp.pad(up_bias[:, None], ((0, 0), (0, 127)))], axis=1)
    packed_z = ring_gather(packed, "z")
    packed_other = lax.ppermute(packed_z, "core", [(0, 1), (1, 0)])
    index = jnp.stack([core, lax.axis_index("z")]).astype(jnp.int32)
    wnat = assemble(index, packed_z, packed_other)

    activated = conv_norm(whole, conv_weight, conv_bias, norm_gain, norm_shift, chips)
    chip_rows = lax.all_to_all(activated, "z", split_axis=0, concat_axis=0, tiled=True)
    chip_rows = chip_rows.reshape(-1, chip_rows.shape[2])
    both = lax.all_gather(chip_rows, "core", axis=0, tiled=True)
    half = coarse.shape[0]
    fine = up_conv(index, both, wnat, half)
    return fine.reshape(2 * half, 2 * width_cols, -1)


def solution(mesh):
    grp, sp = mesh.devices.shape
    fine_mesh = Mesh(mesh.devices.reshape(grp, sp // 2, 2), ("grp", "z", "core"))
    rows = ("grp", "z", "core")
    chans = ("z", "core")
    return jax.shard_map(
        body,
        mesh=fine_mesh,
        in_specs=(
            P(rows, None, None),
            P(chans, None, None, None),
            P(chans),
            P(chans),
            P(chans),
            P(chans, None, None, None),
            P(chans),
        ),
        out_specs=P(rows, None, None),
        check_vma=False,
    )
```

```python
import functools

import jax
import jax.numpy as jnp
from jax import lax
from jax.experimental import pallas as pl
from jax.experimental.pallas import tpu as pltpu
from jax.sharding import Mesh, PartitionSpec as P

GSIZE = 32


def conv_norm_kernel(x_ref, w_ref, bias_ref, gain_ref, shift_ref, out_ref, *, height, width_cols):
    outputs = out_ref.shape[1]
    positions = height * width_cols
    taps = lax.dot_general(w_ref[...], x_ref[...], (((1,), (1,)), ((), ())),
                           preferred_element_type=jnp.float32)
    pos = lax.broadcasted_iota(jnp.int32, (1, positions), 1)
    row = pos // width_cols
    col = pos % width_cols
    acc = jnp.zeros((outputs, positions), jnp.float32)
    for t in range(9):
        r, s = divmod(t, 3)
        off = (r - 1) * width_cols + (s - 1)
        part = taps[t * outputs:(t + 1) * outputs, :]
        if off:
            part = pltpu.roll(part, (-off) % positions, 1)
        valid = ((row + (r - 1) >= 0) & (row + (r - 1) < height)
                 & (col + (s - 1) >= 0) & (col + (s - 1) < width_cols))
        acc = acc + jnp.where(valid, part, 0.0)
    conv = acc + bias_ref[...]
    groups = outputs // GSIZE
    grouped = conv.reshape(groups, GSIZE, positions)
    count = GSIZE * positions
    centre = jnp.sum(jnp.sum(grouped, axis=2, keepdims=True), axis=1, keepdims=True) / count
    dev = grouped - centre
    spread = jnp.sum(jnp.sum(dev * dev, axis=2, keepdims=True), axis=1, keepdims=True) / count
    normed = (dev * lax.rsqrt(spread + 1e-05)).reshape(outputs, positions)
    v = normed * gain_ref[...] + shift_ref[...]
    act = (v / (1.0 + jnp.exp(-v))).astype(out_ref.dtype)
    chips, _, span = out_ref.shape
    for chip in range(chips):
        out_ref[chip] = act[:, chip * span:(chip + 1) * span]


def conv_norm(whole, conv_weight, conv_bias, norm_gain, norm_shift, chips):
    height, width_cols, channels = whole.shape
    outputs = conv_weight.shape[0]
    x = whole.reshape(height * width_cols, channels)
    w = jnp.transpose(conv_weight.reshape(outputs, 9, channels), (1, 0, 2)).reshape(9 * outputs, channels)
    col = lambda v: v.astype(jnp.float32).reshape(outputs, 1)
    vmem = pl.BlockSpec(memory_space=pltpu.VMEM)
    return pl.pallas_call(
        functools.partial(conv_norm_kernel, height=height, width_cols=width_cols),
        out_shape=jax.ShapeDtypeStruct((chips, outputs, height * width_cols // chips), jnp.bfloat16),
        in_specs=[vmem] * 5,
        out_specs=vmem,
        cost_estimate=pl.CostEstimate(
            flops=2 * height * width_cols * channels * 9 * outputs,
            transcendentals=height * width_cols * outputs,
            bytes_accessed=x.size * 2 + w.size * 2 + outputs * height * width_cols * 2),
    )(x, w, col(conv_bias), col(norm_gain), col(norm_shift))


def assemble_kernel(index_ref, own_ref, other_ref, wnat_ref):
    chips, slab, _ = own_ref.shape
    core = index_ref[0]
    here = index_ref[1]
    for m in range(chips):
        chip = (here + m) % chips
        mine = pl.multiple_of(2 * slab * chip + slab * core, slab)
        theirs = pl.multiple_of(2 * slab * chip + slab * (1 - core), slab)
        wnat_ref[pl.ds(mine, slab), :] = own_ref[m]
        wnat_ref[pl.ds(theirs, slab), :] = other_ref[m]


def assemble(index, own, other):
    chips, slab, packed_width = own.shape
    vmem = pl.BlockSpec(memory_space=pltpu.VMEM)
    smem = pl.BlockSpec(memory_space=pltpu.SMEM)
    return pl.pallas_call(
        assemble_kernel,
        out_shape=jax.ShapeDtypeStruct((2 * chips * slab, packed_width), own.dtype),
        in_specs=[smem, vmem, vmem],
        out_specs=vmem,
        cost_estimate=pl.CostEstimate(flops=0, transcendentals=0, bytes_accessed=4 * own.size * 2),
    )(index, own, other)


def up_kernel(index_ref, act_ref, wnat_hbm, out_ref, actn_ref, w_buf, b_buf, sems, *, width_cols):
    outs, packed_width = wnat_hbm.shape
    channels, positions = act_ref.shape
    chips = outs // 32
    block = channels // (2 * chips)
    core = index_ref[0]
    copies = [pltpu.make_async_copy(wnat_hbm.at[:, pl.ds(ab * channels, channels)], w_buf.at[ab], sems.at[ab])
              for ab in range(4)]
    copies.append(pltpu.make_async_copy(wnat_hbm.at[:, pl.ds(4 * channels, packed_width - 4 * channels)],
                                        b_buf, sems.at[4]))
    for copy in copies:
        copy.start()
    rows = out_ref.shape[0] // 2
    span = rows * width_cols
    lanes = actn_ref.shape[1]
    skip = positions - lanes
    for c in range(2):
        for z in range(chips):
            rows_in = act_ref[pl.ds((c * chips + z) * block, block), :]
            actn_ref[pl.ds((2 * z + c) * block, block), :] = jnp.where(core == 0, rows_in[:, :lanes], rows_in[:, skip:])
    nn = (((1,), (0,)), ((), ()))
    sub = lax.broadcasted_iota(jnp.int32, (packed_width - 4 * channels, lanes), 0)
    ones = jnp.where(sub == 0, 1.0, 0.0).astype(actn_ref.dtype)
    copies[4].wait()
    bias = lax.dot_general(b_buf[...], ones, nn, preferred_element_type=jnp.float32)
    act = actn_ref[...]
    first = lanes - span
    dest = lax.broadcasted_iota(jnp.int32, (2 * width_cols, 2 * width_cols), 0)
    src = lax.broadcasted_iota(jnp.int32, (2 * width_cols, 2 * width_cols), 1)
    interleave = jnp.where(src == (dest % 2) * width_cols + dest // 2, 1.0, 0.0).astype(out_ref.dtype)
    for a in range(2):
        phases = []
        for b in range(2):
            copies[2 * a + b].wait()
            res = lax.dot_general(w_buf[2 * a + b], act, nn, preferred_element_type=jnp.float32)
            res = jnp.transpose(res + bias).astype(out_ref.dtype)
            phases.append(jnp.where(core == 0, res[:span], res[first:]))
        for i in range(rows):
            stacked = jnp.concatenate([p[i * width_cols:(i + 1) * width_cols] for p in phases], axis=0)
            out_ref[2 * i + a] = jnp.dot(interleave, stacked, preferred_element_type=jnp.float32).astype(out_ref.dtype)


def up_conv(index, act, wnat, rows):
    channels, positions = act.shape
    width_cols = positions // (2 * rows)
    outs, packed_width = wnat.shape
    vmem = pl.BlockSpec(memory_space=pltpu.VMEM)
    smem = pl.BlockSpec(memory_space=pltpu.SMEM)
    return pl.pallas_call(
        functools.partial(up_kernel, width_cols=width_cols),
        out_shape=jax.ShapeDtypeStruct((2 * rows, 2 * width_cols, outs), jnp.bfloat16),
        in_specs=[smem, vmem, pl.BlockSpec(memory_space=pl.ANY)],
        out_specs=vmem,
        scratch_shapes=[pltpu.VMEM((channels, -(-positions // 2 // 128) * 128), act.dtype),
                        pltpu.VMEM((4, outs, channels), wnat.dtype),
                        pltpu.VMEM((outs, packed_width - 4 * channels), wnat.dtype),
                        pltpu.SemaphoreType.DMA((5,))],
        cost_estimate=pl.CostEstimate(
            flops=2 * positions * channels * 4 * outs, transcendentals=0,
            bytes_accessed=act.size * 2 + wnat.size * 2 + rows * width_cols * 4 * outs * 2),
    )(index, act, wnat)


def ring_gather(block, axis):
    chips = lax.axis_size(axis)
    step_up = [(i, (i - 1) % chips) for i in range(chips)]
    step_down = [(i, (i + 1) % chips) for i in range(chips)]
    ahead, behind = block, block
    from_ahead, from_behind = [], []
    for k in range(1, chips // 2 + 1):
        ahead = lax.ppermute(ahead, axis, step_up)
        from_ahead.append(ahead)
        if k < chips - chips // 2:
            behind = lax.ppermute(behind, axis, step_down)
            from_behind.append(behind)
    return jnp.stack([block] + from_ahead + from_behind[::-1])


def body(coarse, conv_weight, conv_bias, norm_gain, norm_shift, up_weight, up_bias):
    chips = lax.axis_size("z")
    core = lax.axis_index("core")
    _, width_cols, channels = coarse.shape
    outputs = conv_weight.shape[0]
    slice_out = up_weight.shape[0]

    whole = lax.all_gather(coarse, ("z", "core"), axis=0, tiled=True)
    height = whole.shape[0]
    flat = up_weight.reshape(slice_out, -1)
    packed = jnp.concatenate([flat, jnp.pad(up_bias[:, None], ((0, 0), (0, 127)))], axis=1)
    packed_z = ring_gather(packed, "z")
    packed_other = lax.ppermute(packed_z, "core", [(0, 1), (1, 0)])
    index = jnp.stack([core, lax.axis_index("z")]).astype(jnp.int32)
    wnat = assemble(index, packed_z, packed_other)

    activated = conv_norm(whole, conv_weight, conv_bias, norm_gain, norm_shift, chips)
    chip_rows = lax.all_to_all(activated, "z", split_axis=0, concat_axis=0, tiled=True)
    chip_rows = chip_rows.reshape(-1, chip_rows.shape[2])
    both = lax.all_gather(chip_rows, "core", axis=0, tiled=True)
    half = coarse.shape[0]
    fine = up_conv(index, both, wnat, half)
    return fine.reshape(2 * half, 2 * width_cols, -1)


def solution(mesh):
    grp, sp = mesh.devices.shape
    fine_mesh = Mesh(mesh.devices.reshape(grp, sp // 2, 2), ("grp", "z", "core"))
    rows = ("grp", "z", "core")
    chans = ("z", "core")
    return jax.shard_map(
        body,
        mesh=fine_mesh,
        in_specs=(
            P(rows, None, None),
            P(chans, None, None, None),
            P(chans),
            P(chans),
            P(chans),
            P(chans, None, None, None),
            P(chans),
        ),
        out_specs=P(rows, None, None),
        check_vma=False,
    )
```

```python
import functools

import jax
import jax.numpy as jnp
from jax import lax
from jax.experimental import pallas as pl
from jax.experimental.pallas import tpu as pltpu
from jax.sharding import Mesh, PartitionSpec as P

GSIZE = 32


def conv_norm_kernel(x_ref, w_ref, bias_ref, gain_ref, shift_ref, out_ref, *, height, width_cols):
    outputs = out_ref.shape[1]
    positions = height * width_cols
    taps = lax.dot_general(w_ref[...], x_ref[...], (((1,), (1,)), ((), ())),
                           preferred_element_type=jnp.float32)
    pos = lax.broadcasted_iota(jnp.int32, (1, positions), 1)
    posf = pos.astype(jnp.float32)
    col = (posf - width_cols * jnp.floor((posf + 0.5) * (1.0 / width_cols))).astype(jnp.int32)
    acc = jnp.zeros((outputs, positions), jnp.float32)
    for t in range(9):
        r, s = divmod(t, 3)
        off = (r - 1) * width_cols + (s - 1)
        part = taps[t * outputs:(t + 1) * outputs, :]
        if off:
            part = pltpu.roll(part, (-off) % positions, 1)
        valid = ((pos + (r - 1) * width_cols >= 0) & (pos + (r - 1) * width_cols < positions)
                 & (col + (s - 1) >= 0) & (col + (s - 1) < width_cols))
        acc = acc + jnp.where(valid, part, 0.0)
    conv = acc + bias_ref[...]
    groups = outputs // GSIZE
    grouped = conv.reshape(groups, GSIZE, positions)
    count = GSIZE * positions
    centre = jnp.sum(jnp.sum(grouped, axis=2, keepdims=True), axis=1, keepdims=True) / count
    dev = grouped - centre
    spread = jnp.sum(jnp.sum(dev * dev, axis=2, keepdims=True), axis=1, keepdims=True) / count
    normed = (dev * lax.rsqrt(spread + 1e-05)).reshape(outputs, positions)
    v = normed * gain_ref[...] + shift_ref[...]
    act = (v / (1.0 + jnp.exp(-v))).astype(out_ref.dtype)
    chips, _, span = out_ref.shape
    for chip in range(chips):
        out_ref[chip] = act[:, chip * span:(chip + 1) * span]


def conv_norm(whole, conv_weight, conv_bias, norm_gain, norm_shift, chips):
    height, width_cols, channels = whole.shape
    outputs = conv_weight.shape[0]
    x = whole.reshape(height * width_cols, channels)
    w = jnp.transpose(conv_weight.reshape(outputs, 9, channels), (1, 0, 2)).reshape(9 * outputs, channels)
    col = lambda v: v.astype(jnp.float32).reshape(outputs, 1)
    vmem = pl.BlockSpec(memory_space=pltpu.VMEM)
    return pl.pallas_call(
        functools.partial(conv_norm_kernel, height=height, width_cols=width_cols),
        out_shape=jax.ShapeDtypeStruct((chips, outputs, height * width_cols // chips), jnp.bfloat16),
        in_specs=[vmem] * 5,
        out_specs=vmem,
        cost_estimate=pl.CostEstimate(
            flops=2 * height * width_cols * channels * 9 * outputs,
            transcendentals=height * width_cols * outputs,
            bytes_accessed=x.size * 2 + w.size * 2 + outputs * height * width_cols * 2),
    )(x, w, col(conv_bias), col(norm_gain), col(norm_shift))


def assemble_kernel(index_ref, own_ref, other_ref, wnat_ref):
    chips, slab, _ = own_ref.shape
    core = index_ref[0]
    here = index_ref[1]
    for m in range(chips):
        chip = (here + m) % chips
        mine = pl.multiple_of(2 * slab * chip + slab * core, slab)
        theirs = pl.multiple_of(2 * slab * chip + slab * (1 - core), slab)
        wnat_ref[pl.ds(mine, slab), :] = own_ref[m]
        wnat_ref[pl.ds(theirs, slab), :] = other_ref[m]


def assemble(index, own, other):
    chips, slab, packed_width = own.shape
    vmem = pl.BlockSpec(memory_space=pltpu.VMEM)
    smem = pl.BlockSpec(memory_space=pltpu.SMEM)
    return pl.pallas_call(
        assemble_kernel,
        out_shape=jax.ShapeDtypeStruct((2 * chips * slab, packed_width), own.dtype),
        in_specs=[smem, vmem, vmem],
        out_specs=vmem,
        cost_estimate=pl.CostEstimate(flops=0, transcendentals=0, bytes_accessed=4 * own.size * 2),
    )(index, own, other)


def up_kernel(index_ref, act_ref, wnat_ref, out_ref, actn_ref, *, width_cols):
    outs, packed_width = wnat_ref.shape
    channels, positions = act_ref.shape
    chips = outs // 32
    block = channels // (2 * chips)
    core = index_ref[0]
    rows = out_ref.shape[0] // 2
    span = rows * width_cols
    lanes = actn_ref.shape[1]
    skip = positions - lanes
    for c in range(2):
        for z in range(chips):
            rows_in = act_ref[pl.ds((c * chips + z) * block, block), :]
            actn_ref[pl.ds((2 * z + c) * block, block), :] = jnp.where(core == 0, rows_in[:, :lanes], rows_in[:, skip:])
    nn = (((1,), (0,)), ((), ()))
    sub = lax.broadcasted_iota(jnp.int32, (packed_width - 4 * channels, lanes), 0)
    ones = jnp.where(sub == 0, 1.0, 0.0).astype(actn_ref.dtype)
    bias = lax.dot_general(wnat_ref[:, pl.ds(4 * channels, packed_width - 4 * channels)], ones, nn,
                           preferred_element_type=jnp.float32)
    act = actn_ref[...]
    first = lanes - span
    dest = lax.broadcasted_iota(jnp.int32, (2 * width_cols, 2 * width_cols), 0)
    src = lax.broadcasted_iota(jnp.int32, (2 * width_cols, 2 * width_cols), 1)
    interleave = jnp.where(src == (dest % 2) * width_cols + dest // 2, 1.0, 0.0).astype(out_ref.dtype)
    for a in range(2):
        phases = []
        for b in range(2):
            res = lax.dot_general(wnat_ref[:, pl.ds((2 * a + b) * channels, channels)], act, nn,
                                  preferred_element_type=jnp.float32)
            res = jnp.transpose(res + bias).astype(out_ref.dtype)
            phases.append(jnp.where(core == 0, res[:span], res[first:]))
        for i in range(rows):
            stacked = jnp.concatenate([p[i * width_cols:(i + 1) * width_cols] for p in phases], axis=0)
            out_ref[2 * i + a] = jnp.dot(interleave, stacked, preferred_element_type=jnp.float32).astype(out_ref.dtype)


def up_conv(index, act, wnat, rows):
    channels, positions = act.shape
    width_cols = positions // (2 * rows)
    outs, packed_width = wnat.shape
    vmem = pl.BlockSpec(memory_space=pltpu.VMEM)
    smem = pl.BlockSpec(memory_space=pltpu.SMEM)
    return pl.pallas_call(
        functools.partial(up_kernel, width_cols=width_cols),
        out_shape=jax.ShapeDtypeStruct((2 * rows, 2 * width_cols, outs), jnp.bfloat16),
        in_specs=[smem, vmem, vmem],
        out_specs=vmem,
        scratch_shapes=[pltpu.VMEM((channels, -(-positions // 2 // 128) * 128), act.dtype)],
        cost_estimate=pl.CostEstimate(
            flops=2 * positions * channels * 4 * outs, transcendentals=0,
            bytes_accessed=act.size * 2 + wnat.size * 2 + rows * width_cols * 4 * outs * 2),
    )(index, act, wnat)


def ring_gather(block, axis):
    chips = lax.axis_size(axis)
    step_up = [(i, (i - 1) % chips) for i in range(chips)]
    step_down = [(i, (i + 1) % chips) for i in range(chips)]
    ahead, behind = block, block
    from_ahead, from_behind = [], []
    for k in range(1, chips // 2 + 1):
        ahead = lax.ppermute(ahead, axis, step_up)
        from_ahead.append(ahead)
        if k < chips - chips // 2:
            behind = lax.ppermute(behind, axis, step_down)
            from_behind.append(behind)
    return jnp.stack([block] + from_ahead + from_behind[::-1])


def body(coarse, conv_weight, conv_bias, norm_gain, norm_shift, up_weight, up_bias):
    chips = lax.axis_size("z")
    core = lax.axis_index("core")
    _, width_cols, channels = coarse.shape
    outputs = conv_weight.shape[0]
    slice_out = up_weight.shape[0]

    whole = lax.all_gather(coarse, ("z", "core"), axis=0, tiled=True)
    height = whole.shape[0]
    flat = up_weight.reshape(slice_out, -1)
    packed = jnp.concatenate([flat, jnp.pad(up_bias[:, None], ((0, 0), (0, 127)))], axis=1)
    packed_z = ring_gather(packed, "z")
    packed_other = lax.ppermute(packed_z, "core", [(0, 1), (1, 0)])
    index = jnp.stack([core, lax.axis_index("z")]).astype(jnp.int32)
    wnat = assemble(index, packed_z, packed_other)

    activated = conv_norm(whole, conv_weight, conv_bias, norm_gain, norm_shift, chips)
    chip_rows = lax.all_to_all(activated, "z", split_axis=0, concat_axis=0, tiled=True)
    chip_rows = chip_rows.reshape(-1, chip_rows.shape[2])
    both = lax.all_gather(chip_rows, "core", axis=0, tiled=True)
    half = coarse.shape[0]
    fine = up_conv(index, both, wnat, half)
    return fine.reshape(2 * half, 2 * width_cols, -1)


def solution(mesh):
    grp, sp = mesh.devices.shape
    fine_mesh = Mesh(mesh.devices.reshape(grp, sp // 2, 2), ("grp", "z", "core"))
    rows = ("grp", "z", "core")
    chans = ("z", "core")
    return jax.shard_map(
        body,
        mesh=fine_mesh,
        in_specs=(
            P(rows, None, None),
            P(chans, None, None, None),
            P(chans),
            P(chans),
            P(chans),
            P(chans, None, None, None),
            P(chans),
        ),
        out_specs=P(rows, None, None),
        check_vma=False,
    )
```

```python
import functools

import jax
import jax.numpy as jnp
from jax import lax
from jax.experimental import pallas as pl
from jax.experimental.pallas import tpu as pltpu
from jax.sharding import Mesh, PartitionSpec as P

GSIZE = 32


def conv_norm_kernel(x_ref, w_ref, bias_ref, gain_ref, shift_ref, out_ref, *, height, width_cols):
    outputs = out_ref.shape[1]
    positions = height * width_cols
    taps = lax.dot_general(w_ref[...], x_ref[...], (((1,), (1,)), ((), ())),
                           preferred_element_type=jnp.float32)
    pos = lax.broadcasted_iota(jnp.int32, (1, positions), 1)
    row = pos // width_cols
    col = pos % width_cols
    acc = jnp.zeros((outputs, positions), jnp.float32)
    for t in range(9):
        r, s = divmod(t, 3)
        off = (r - 1) * width_cols + (s - 1)
        part = taps[t * outputs:(t + 1) * outputs, :]
        if off:
            part = pltpu.roll(part, (-off) % positions, 1)
        valid = ((row + (r - 1) >= 0) & (row + (r - 1) < height)
                 & (col + (s - 1) >= 0) & (col + (s - 1) < width_cols))
        acc = acc + jnp.where(valid, part, 0.0)
    conv = acc + bias_ref[...]
    groups = outputs // GSIZE
    grouped = conv.reshape(groups, GSIZE, positions)
    count = GSIZE * positions
    centre = jnp.sum(jnp.sum(grouped, axis=2, keepdims=True), axis=1, keepdims=True) / count
    dev = grouped - centre
    spread = jnp.sum(jnp.sum(dev * dev, axis=2, keepdims=True), axis=1, keepdims=True) / count
    normed = (dev * lax.rsqrt(spread + 1e-05)).reshape(outputs, positions)
    v = normed * gain_ref[...] + shift_ref[...]
    act = (v * (0.5 + 0.5 * jnp.tanh(0.5 * v))).astype(out_ref.dtype)
    chips, _, span = out_ref.shape
    for chip in range(chips):
        out_ref[chip] = act[:, chip * span:(chip + 1) * span]


def conv_norm(whole, conv_weight, conv_bias, norm_gain, norm_shift, chips):
    height, width_cols, channels = whole.shape
    outputs = conv_weight.shape[0]
    x = whole.reshape(height * width_cols, channels)
    w = jnp.transpose(conv_weight.reshape(outputs, 9, channels), (1, 0, 2)).reshape(9 * outputs, channels)
    col = lambda v: v.astype(jnp.float32).reshape(outputs, 1)
    vmem = pl.BlockSpec(memory_space=pltpu.VMEM)
    return pl.pallas_call(
        functools.partial(conv_norm_kernel, height=height, width_cols=width_cols),
        out_shape=jax.ShapeDtypeStruct((chips, outputs, height * width_cols // chips), jnp.bfloat16),
        in_specs=[vmem] * 5,
        out_specs=vmem,
        cost_estimate=pl.CostEstimate(
            flops=2 * height * width_cols * channels * 9 * outputs,
            transcendentals=height * width_cols * outputs,
            bytes_accessed=x.size * 2 + w.size * 2 + outputs * height * width_cols * 2),
    )(x, w, col(conv_bias), col(norm_gain), col(norm_shift))


def assemble_kernel(index_ref, own_ref, other_ref, wnat_ref):
    chips, slab, _ = own_ref.shape
    core = index_ref[0]
    here = index_ref[1]
    for m in range(chips):
        chip = (here + m) % chips
        mine = pl.multiple_of(2 * slab * chip + slab * core, slab)
        theirs = pl.multiple_of(2 * slab * chip + slab * (1 - core), slab)
        wnat_ref[pl.ds(mine, slab), :] = own_ref[m]
        wnat_ref[pl.ds(theirs, slab), :] = other_ref[m]


def assemble(index, own, other):
    chips, slab, packed_width = own.shape
    vmem = pl.BlockSpec(memory_space=pltpu.VMEM)
    smem = pl.BlockSpec(memory_space=pltpu.SMEM)
    return pl.pallas_call(
        assemble_kernel,
        out_shape=jax.ShapeDtypeStruct((2 * chips * slab, packed_width), own.dtype),
        in_specs=[smem, vmem, vmem],
        out_specs=vmem,
        cost_estimate=pl.CostEstimate(flops=0, transcendentals=0, bytes_accessed=4 * own.size * 2),
    )(index, own, other)


def up_kernel(index_ref, act_ref, wnat_ref, out_ref, actn_ref, *, width_cols):
    outs, packed_width = wnat_ref.shape
    channels, positions = act_ref.shape
    chips = outs // 32
    block = channels // (2 * chips)
    core = index_ref[0]
    rows = out_ref.shape[0] // 2
    span = rows * width_cols
    lanes = actn_ref.shape[1]
    skip = positions - lanes
    for c in range(2):
        for z in range(chips):
            rows_in = act_ref[pl.ds((c * chips + z) * block, block), :]
            actn_ref[pl.ds((2 * z + c) * block, block), :] = jnp.where(core == 0, rows_in[:, :lanes], rows_in[:, skip:])
    nn = (((1,), (0,)), ((), ()))
    sub = lax.broadcasted_iota(jnp.int32, (packed_width - 4 * channels, lanes), 0)
    ones = jnp.where(sub == 0, 1.0, 0.0).astype(actn_ref.dtype)
    bias = lax.dot_general(wnat_ref[:, pl.ds(4 * channels, packed_width - 4 * channels)], ones, nn,
                           preferred_element_type=jnp.float32)
    act = actn_ref[...]
    first = lanes - span
    dest = lax.broadcasted_iota(jnp.int32, (2 * width_cols, 2 * width_cols), 0)
    src = lax.broadcasted_iota(jnp.int32, (2 * width_cols, 2 * width_cols), 1)
    interleave = jnp.where(src == (dest % 2) * width_cols + dest // 2, 1.0, 0.0).astype(out_ref.dtype)
    for a in range(2):
        phases = []
        for b in range(2):
            res = lax.dot_general(wnat_ref[:, pl.ds((2 * a + b) * channels, channels)], act, nn,
                                  preferred_element_type=jnp.float32)
            res = jnp.transpose(res + bias).astype(out_ref.dtype)
            phases.append(jnp.where(core == 0, res[:span], res[first:]))
        for i in range(rows):
            stacked = jnp.concatenate([p[i * width_cols:(i + 1) * width_cols] for p in phases], axis=0)
            out_ref[2 * i + a] = jnp.dot(interleave, stacked, preferred_element_type=jnp.float32).astype(out_ref.dtype)


def up_conv(index, act, wnat, rows):
    channels, positions = act.shape
    width_cols = positions // (2 * rows)
    outs, packed_width = wnat.shape
    vmem = pl.BlockSpec(memory_space=pltpu.VMEM)
    smem = pl.BlockSpec(memory_space=pltpu.SMEM)
    return pl.pallas_call(
        functools.partial(up_kernel, width_cols=width_cols),
        out_shape=jax.ShapeDtypeStruct((2 * rows, 2 * width_cols, outs), jnp.bfloat16),
        in_specs=[smem, vmem, vmem],
        out_specs=vmem,
        scratch_shapes=[pltpu.VMEM((channels, -(-positions // 2 // 128) * 128), act.dtype)],
        cost_estimate=pl.CostEstimate(
            flops=2 * positions * channels * 4 * outs, transcendentals=0,
            bytes_accessed=act.size * 2 + wnat.size * 2 + rows * width_cols * 4 * outs * 2),
    )(index, act, wnat)


def ring_gather(block, axis):
    chips = lax.axis_size(axis)
    step_up = [(i, (i - 1) % chips) for i in range(chips)]
    step_down = [(i, (i + 1) % chips) for i in range(chips)]
    ahead, behind = block, block
    from_ahead, from_behind = [], []
    for k in range(1, chips // 2 + 1):
        ahead = lax.ppermute(ahead, axis, step_up)
        from_ahead.append(ahead)
        if k < chips - chips // 2:
            behind = lax.ppermute(behind, axis, step_down)
            from_behind.append(behind)
    return jnp.stack([block] + from_ahead + from_behind[::-1])


def body(coarse, conv_weight, conv_bias, norm_gain, norm_shift, up_weight, up_bias):
    chips = lax.axis_size("z")
    core = lax.axis_index("core")
    _, width_cols, channels = coarse.shape
    outputs = conv_weight.shape[0]
    slice_out = up_weight.shape[0]

    whole = lax.all_gather(coarse, ("z", "core"), axis=0, tiled=True)
    height = whole.shape[0]
    flat = up_weight.reshape(slice_out, -1)
    packed = jnp.concatenate([flat, jnp.pad(up_bias[:, None], ((0, 0), (0, 127)))], axis=1)
    packed_z = ring_gather(packed, "z")
    packed_other = lax.ppermute(packed_z, "core", [(0, 1), (1, 0)])
    index = jnp.stack([core, lax.axis_index("z")]).astype(jnp.int32)
    wnat = assemble(index, packed_z, packed_other)

    activated = conv_norm(whole, conv_weight, conv_bias, norm_gain, norm_shift, chips)
    chip_rows = lax.all_to_all(activated, "z", split_axis=0, concat_axis=0, tiled=True)
    chip_rows = chip_rows.reshape(-1, chip_rows.shape[2])
    both = lax.all_gather(chip_rows, "core", axis=0, tiled=True)
    half = coarse.shape[0]
    fine = up_conv(index, both, wnat, half)
    return fine.reshape(2 * half, 2 * width_cols, -1)


def solution(mesh):
    grp, sp = mesh.devices.shape
    fine_mesh = Mesh(mesh.devices.reshape(grp, sp // 2, 2), ("grp", "z", "core"))
    rows = ("grp", "z", "core")
    chans = ("z", "core")
    return jax.shard_map(
        body,
        mesh=fine_mesh,
        in_specs=(
            P(rows, None, None),
            P(chans, None, None, None),
            P(chans),
            P(chans),
            P(chans),
            P(chans, None, None, None),
            P(chans),
        ),
        out_specs=P(rows, None, None),
        check_vma=False,
    )
```
